128 devices in a mesh: dp: 4 (over x), lat: 4 (over z), lon: 8 (over y, core).
Axes of the slice: x: 4, y: 4, z: 4, core: 2. Of those that a mesh axis runs over, the one named last changes fastest.
Arguments:
- grid_feat: bfloat16 [128, 2048, 474], P(('dp', 'lat'), 'lon'), parts along dimension 0, may hold values from -6 to 6
- mesh_in: bfloat16 [256, 256, 512], P(('dp', 'lat'), 'lon'), parts along dimension 0, may hold values from -6 to 6
- w_grid: bfloat16 [474, 512], replicated, may hold values from -0.25 to 0.25
- w_src: bfloat16 [512, 512], replicated, may hold values from -0.25 to 0.25
- w_dst: bfloat16 [512, 512], replicated, may hold values from -0.25 to 0.25
- b_edge: float32 [512], replicated, may hold values from -3 to 3
- w_node: bfloat16 [512, 512], replicated, may hold values from -0.25 to 0.25
- node_gain: float32 [512], replicated, may hold values from 0.5 to 1.5
- mix_gain: float32 [512], replicated, may hold values from 0.2 to 0.8
- send_rows: int32 [128, 32, 256], P(('dp', 'lat', 'lon')), parts along dimension 0, may hold values from 0 to 2047
- send_target: int32 [128, 32, 256], P(('dp', 'lat', 'lon')), parts along dimension 0, may hold values from 0 to 511
- send_counts: int32 [128, 32], P(('dp', 'lat', 'lon')), parts along dimension 0, may hold values from 0 to 256, as said below
- local_rows: int32 [128, 2048], P(('dp', 'lat', 'lon')), parts along dimension 0, may hold values from 0 to 2047
- local_target: int32 [128, 2048], P(('dp', 'lat', 'lon')), parts along dimension 0, may hold values from 0 to 511
- local_counts: int32 [128], P(('dp', 'lat', 'lon')), parts along dimension 0, may hold values from 1024 to 2048, as said below
- cotangent: bfloat16 [256, 256, 512], P(('dp', 'lat'), 'lon'), parts along dimension 0, may hold values from -6 to 6
Outputs:
- mesh_out: float32 [256, 256, 512], P(('dp', 'lat'), 'lon'), parts along dimension 0
- grad_grid: float32 [1896, 512], P('dp', ('lat', 'lon')), parts along dimension 0
- grad_src: float32 [2048, 512], P('dp', ('lat', 'lon')), parts along dimension 0
- grad_dst: float32 [2048, 512], P('dp', ('lat', 'lon')), parts along dimension 0
- grad_node: float32 [2048, 512], P('dp', ('lat', 'lon')), parts along dimension 0
The draws below stay inside these ranges and needn't reach their ends.
There are 4 independent parts, one for each index of `dp`. The reference program is written for one: setup_inputs(seed, part) draws one part's arguments, and reference() takes and returns one part's arrays. A program takes and returns all parts, laid end to end along the dimension named above; an argument that names none is the same for every part. Nothing has to cross between parts.
Inputs may be any that keep to these rules, and one draw needn't show every extreme that they name: send_counts[s, p] is the number of leading slots of send_rows[s, p] and send_target[s, p] that are edges; it is 0 unless p differs from s and the latitude indices of the tiles differ by at most one and their longitude indices by at most one around the cycle; it equals 256 somewhere in every draw. local_counts[p] is the number of leading entries of local_rows[p] and local_target[p] that are edges; it equals 2048 somewhere in every draw.
All inputs are finite; a program needn't handle non-finite values.
Results may differ from the reference program's by a relative error of at most 0.015.
Values may be sent and summed in bfloat16 or wider, within the bound.
No kernel may reach another device: no remote copies, remote signals or barrier semaphores. Data moves between devices by JAX's collectives and lax.ppermute only.
A program may use at most 128 MiB of HBM per device.

```python
import jax
import jax.numpy as jnp
import numpy as np
from jax import lax

C = 474
L = 512
RLAT = 8
RLON = 256
MLAT = 16
MLON = 32
CAP = 256
EL = 2048
PEERS = 32
GLAT = 32
GLON = 2048
MESH_LAT = 64
MESH_LON = 256
N_LAT = 4
N_LON = 8


def draw_send_counts(key, part):
    peer_count = N_LAT * N_LON
    source_tile = jnp.arange(peer_count, dtype=jnp.int32)[:, None]
    target_tile = jnp.arange(peer_count, dtype=jnp.int32)[None, :]
    source_lat = source_tile // N_LON
    target_lat = target_tile // N_LON
    lon_gap = (target_tile % N_LON - source_tile % N_LON) % N_LON
    nearby = (jnp.abs(target_lat - source_lat) <= 1) & ((lon_gap <= 1) | (lon_gap == N_LON - 1)) & (source_tile != target_tile)
    polar = (source_lat == 0) | (source_lat == N_LAT - 1)
    first_key, second_key, third_key = jax.random.split(jax.random.fold_in(key, 7), 3)
    heavy = jax.random.randint(first_key, (peer_count, peer_count), CAP // 2, CAP + 1)
    light = jax.random.randint(second_key, (peer_count, peer_count), CAP // 8, CAP // 2 + 1)
    counts = jnp.where(polar, heavy, light)
    chosen = jax.random.randint(third_key, (), 0, peer_count)
    chosen_lat = chosen // N_LON
    partner_lat = jnp.where(chosen_lat + 1 < N_LAT, chosen_lat + 1, chosen_lat - 1)
    partner = partner_lat * N_LON + chosen % N_LON
    counts = jnp.where((source_tile == chosen) & (target_tile == partner), CAP, counts)
    return jnp.where(nearby, counts, 0).astype(jnp.int32)


def draw_local_counts(key, part):
    peer_count = N_LAT * N_LON
    first_key, second_key = jax.random.split(jax.random.fold_in(key, 11))
    counts = jax.random.randint(first_key, (peer_count,), EL // 2, EL + 1)
    chosen = jax.random.randint(second_key, (), 0, peer_count)
    return jnp.where(jnp.arange(peer_count, dtype=jnp.int32) == chosen, EL, counts).astype(jnp.int32)


def plant(array, stream_key, least, high):
    longest = array.shape.index(max(array.shape))
    spots = []
    for shift in (0, 1):
        where = [jax.random.randint(jax.random.fold_in(stream_key, axis), (), 0, length) for axis, length in enumerate(array.shape)]
        where[longest] = (where[longest] + shift) % array.shape[longest]
        spots.append(tuple(where))
    return array.at[spots[0]].set(least).at[spots[1]].set(high)


def level_of(stream_key, dims, pieces, smallest, largest):
    gain, own = 1.0, jax.random.fold_in(stream_key, 6)
    for dim, blocks in pieces:
        steps = jnp.exp(jax.random.uniform(jax.random.fold_in(own, dim), (blocks,), jnp.float32, smallest / len(pieces), largest / len(pieces)))
        gain = gain * jnp.repeat(steps, dims[dim] // blocks).reshape([-1 if axis == dim else 1 for axis in range(len(dims))])
    return gain


def noise(key, dims, scale, most, cuts=(), kind=jnp.bfloat16):
    loudness = level_of(key, dims, cuts, -0.22, 0.18) if cuts else 1.0
    array = jax.random.normal(key, dims, jnp.float32) * scale * loudness
    return jnp.minimum(jnp.maximum(array, -most), most).astype(kind)


def setup_inputs(seed: int = 0, part: int = 0) -> dict:
    keys = jax.random.split(jax.random.key(seed), 17)
    part_keys = jax.random.split(jax.random.fold_in(keys[16], part), 17)
    grid_feat = noise(part_keys[0], (GLAT, GLON, C), 1.0, 6.0, ((0, 4), (1, 8)))
    mesh_in = noise(part_keys[1], (MESH_LAT, MESH_LON, L), 1.0, 6.0, ((0, 4), (1, 8)))
    w_grid = noise(keys[2], (C, L), C ** -0.5, 0.25)
    w_src = noise(keys[3], (L, L), L ** -0.5, 0.25)
    w_dst = noise(keys[4], (L, L), L ** -0.5, 0.25)
    b_edge = noise(keys[5], (L,), 0.5, 3.0, (), jnp.float32)
    w_node = noise(keys[6], (L, L), L ** -0.5, 0.25)
    node_gain = jnp.clip(1.0 + 0.1 * jax.random.normal(keys[7], (L,), jnp.float32), 0.5, 1.5)
    mix_gain = jnp.clip(jax.random.uniform(keys[8], (L,), jnp.float32, 0.2, 0.8), 0.2, 0.8)
    send_rows = plant(jax.random.randint(part_keys[9], (PEERS, PEERS, CAP), 0, RLAT * RLON), jax.random.fold_in(part_keys[9], 1), 0, (RLAT * RLON) - 1).astype(jnp.int32)
    send_target = plant(jax.random.randint(part_keys[10], (PEERS, PEERS, CAP), 0, MLAT * MLON), jax.random.fold_in(part_keys[10], 1), 0, (MLAT * MLON) - 1).astype(jnp.int32)
    send_counts = draw_send_counts(jax.random.fold_in(jax.random.fold_in(keys[16], part), 71), part)
    local_rows = plant(jax.random.randint(part_keys[12], (PEERS, EL), 0, RLAT * RLON), jax.random.fold_in(part_keys[12], 1), 0, (RLAT * RLON) - 1).astype(jnp.int32)
    local_target = plant(jax.random.randint(part_keys[13], (PEERS, EL), 0, MLAT * MLON), jax.random.fold_in(part_keys[13], 1), 0, (MLAT * MLON) - 1).astype(jnp.int32)
    local_counts = draw_local_counts(jax.random.fold_in(jax.random.fold_in(keys[16], part), 71), part)
    cotangent = noise(part_keys[15], (MESH_LAT, MESH_LON, L), 1.0, 6.0, ((0, 4), (1, 8)))
    return {"grid_feat": grid_feat, "mesh_in": mesh_in, "w_grid": w_grid, "w_src": w_src, "w_dst": w_dst, "b_edge": b_edge, "w_node": w_node, "node_gain": node_gain, "mix_gain": mix_gain, "send_rows": send_rows, "send_target": send_target, "send_counts": send_counts, "local_rows": local_rows, "local_target": local_target, "local_counts": local_counts, "cotangent": cotangent}


LAYER_EPSILON = 1e-05

def silu_slope(values):
    sigmoid_part = jax.nn.sigmoid(values)
    return sigmoid_part * (1.0 + values * (1.0 - sigmoid_part))

def tiles_first(whole, tile_a, tile_b):
    channels = whole.shape[-1]
    blocks = whole.reshape(N_LAT, tile_a, N_LON, tile_b, channels)
    return blocks.transpose(0, 2, 1, 3, 4).reshape(N_LAT * N_LON, tile_a * tile_b, channels)

def tiles_back(tiled, tile_a, tile_b):
    channels = tiled.shape[-1]
    blocks = tiled.reshape(N_LAT, N_LON, tile_a, tile_b, channels)
    return blocks.transpose(0, 2, 1, 3, 4).reshape(N_LAT * tile_a, N_LON * tile_b, channels)

def cycle_mix(mesh_field):
    above = jnp.pad(mesh_field[1:], ((0, 1), (0, 0), (0, 0)))
    below = jnp.pad(mesh_field[:-1], ((1, 0), (0, 0), (0, 0)))
    return 0.25 * (above + below + jnp.roll(mesh_field, 1, axis=1) + jnp.roll(mesh_field, -1, axis=1))

def neighbour_table():
    lat_steps = [lat_step for lat_step in (-1, 0, 1) if abs(lat_step) < N_LAT]
    lon_steps = sorted(set((lon_step % N_LON for lon_step in (-1, 0, 1))))
    offsets = [(lat_step, lon_step) for lat_step in lat_steps for lon_step in lon_steps if (lat_step, lon_step) != (0, 0)]
    peer_count = N_LAT * N_LON
    source_table = np.zeros((peer_count, len(offsets)), np.int32)
    usable = np.zeros((peer_count, len(offsets)), np.float32)
    for target_tile in range(peer_count):
        tile_row = target_tile // N_LON
        tile_column = target_tile % N_LON
        for position, (lat_step, lon_step) in enumerate(offsets):
            source_row = tile_row - lat_step
            if 0 <= source_row < N_LAT:
                source_table[target_tile, position] = source_row * N_LON + (tile_column - lon_step) % N_LON
                usable[target_tile, position] = 1.0
    return (source_table, usable)

def reference(grid_feat, mesh_in, w_grid, w_src, w_dst, b_edge, w_node, node_gain, mix_gain, send_rows, send_target, send_counts, local_rows, local_target, local_counts, cotangent):
    peer_count = N_LAT * N_LON
    tile_rows = RLAT * RLON
    tile_nodes = MLAT * MLON
    features = tiles_first(grid_feat, RLAT, RLON).reshape(-1, C)
    mesh_tiles = tiles_first(mesh_in, MLAT, MLON)
    mesh_flat = mesh_tiles.reshape(-1, L)
    grid_pre = jnp.dot(features, w_grid, preferred_element_type=jnp.float32)
    grid_latent = jax.nn.silu(grid_pre).astype(jnp.bfloat16)
    queries = jnp.dot(mesh_flat, w_dst, preferred_element_type=jnp.float32).reshape(peer_count, tile_nodes, L)
    source_table, usable = neighbour_table()
    remote_sources = jnp.asarray(source_table).astype(jnp.int32)
    usable_tiles = jnp.asarray(usable).astype(jnp.float32)
    dest_ids = jnp.arange(peer_count, dtype=jnp.int32)
    slot_ids = jnp.arange(CAP, dtype=jnp.int32)
    local_senders = dest_ids[:, None] * tile_rows + local_rows
    local_valid = (jnp.arange(EL, dtype=jnp.int32)[None, :] < local_counts[:, None]).astype(jnp.float32)
    remote_rows = send_rows[remote_sources, dest_ids[:, None], :]
    remote_senders = remote_sources[:, :, None] * tile_rows + remote_rows
    remote_targets = send_target[remote_sources, dest_ids[:, None], :]
    remote_counts = send_counts[remote_sources, dest_ids[:, None]]
    remote_valid = (slot_ids[None, None, :] < remote_counts[:, :, None]).astype(jnp.float32) * usable_tiles[:, :, None]
    edge_senders = jnp.concatenate([local_senders, remote_senders.reshape(peer_count, -1)], axis=1).astype(jnp.int32)
    edge_targets = jnp.concatenate([local_target, remote_targets.reshape(peer_count, -1)], axis=1).astype(jnp.int32)
    edge_mask = jnp.concatenate([local_valid, remote_valid.reshape(peer_count, -1)], axis=1)

    def messages_of(senders, targets, valid, query_tile):
        gathered = grid_latent[senders]
        pre_edge = jnp.dot(gathered, w_src, preferred_element_type=jnp.float32) + query_tile[targets] + b_edge
        message = (jax.nn.silu(pre_edge) * valid[:, None]).astype(jnp.bfloat16)
        return (gathered, pre_edge, message)

    def forward_tile(packed):
        senders, targets, valid, query_tile = packed
        message = messages_of(senders, targets, valid, query_tile)[2]
        return jax.ops.segment_sum(message.astype(jnp.float32), targets, num_segments=tile_nodes)
    aggregate = lax.map(forward_tile, (edge_senders, edge_targets, edge_mask, queries))
    aggregate_b = aggregate.reshape(-1, L).astype(jnp.bfloat16)
    hidden = jnp.dot(aggregate_b, w_node, preferred_element_type=jnp.float32)
    active = jax.nn.silu(hidden)
    row_mean = lax.optimization_barrier(jnp.mean(active, axis=-1, keepdims=True))
    centred = active - row_mean
    inverse_scale = lax.rsqrt(lax.optimization_barrier(jnp.mean(centred * centred, axis=-1, keepdims=True)) + LAYER_EPSILON)
    normed = centred * inverse_scale
    updated = (mesh_flat.astype(jnp.float32) + normed * node_gain).astype(jnp.bfloat16)
    updated_field = tiles_back(updated.reshape(peer_count, tile_nodes, L), MLAT, MLON).astype(jnp.float32)
    mesh_out = updated_field + mix_gain * cycle_mix(updated_field)
    cot_values = cotangent.astype(jnp.float32)
    mixed_cot = (mix_gain * cot_values).astype(jnp.bfloat16)
    d_updated = cot_values + cycle_mix(mixed_cot.astype(jnp.float32))
    scaled_grad = tiles_first(d_updated, MLAT, MLON).reshape(-1, L) * node_gain
    d_active = inverse_scale * (scaled_grad - lax.optimization_barrier(jnp.mean(scaled_grad, axis=-1, keepdims=True)) - normed * lax.optimization_barrier(jnp.mean(scaled_grad * normed, axis=-1, keepdims=True)))
    d_hidden = (d_active * silu_slope(hidden)).astype(jnp.bfloat16)
    grad_node = jnp.dot(aggregate_b.T, d_hidden, preferred_element_type=jnp.float32)
    d_aggregate = jnp.dot(d_hidden, w_node.T, preferred_element_type=jnp.float32).astype(jnp.bfloat16).reshape(peer_count, tile_nodes, L)

    def backward_tile(packed):
        senders, targets, valid, query_tile, d_agg_tile = packed
        gathered, pre_edge, unused_message = messages_of(senders, targets, valid, query_tile)
        d_message = d_agg_tile[targets]
        d_pre = (d_message.astype(jnp.float32) * silu_slope(pre_edge) * valid[:, None]).astype(jnp.bfloat16)
        grad_part = jnp.dot(gathered.T, d_pre, preferred_element_type=jnp.float32)
        d_gathered = jnp.dot(d_pre, w_src.T, preferred_element_type=jnp.float32).astype(jnp.bfloat16)
        d_query = jax.ops.segment_sum(d_pre.astype(jnp.float32), targets, num_segments=tile_nodes).astype(jnp.bfloat16)
        return (grad_part, d_gathered, d_query)
    grad_parts, d_gathered, d_query = lax.map(backward_tile, (edge_senders, edge_targets, edge_mask, queries, d_aggregate))
    grad_src = lax.optimization_barrier(jnp.sum(grad_parts, axis=0))
    grad_dst = jnp.dot(mesh_flat.T, d_query.reshape(-1, L), preferred_element_type=jnp.float32)
    d_grid = jax.ops.segment_sum(d_gathered.reshape(-1, L).astype(jnp.float32), edge_senders.reshape(-1), num_segments=peer_count * tile_rows)
    d_grid_pre = (d_grid * silu_slope(grid_pre)).astype(jnp.bfloat16)
    grad_grid = jnp.dot(features.T, d_grid_pre, preferred_element_type=jnp.float32)
    return (mesh_out, grad_grid, grad_src, grad_dst, grad_node)
```

```python
import functools

import jax
import jax.numpy as jnp
from jax import lax
from jax.experimental import pallas as pl
from jax.experimental.pallas import tpu as pltpu
from jax.sharding import PartitionSpec as P

LAYER_EPSILON = 1e-05
F32 = jnp.float32
BF16 = jnp.bfloat16
VMEM = pl.BlockSpec(memory_space=pltpu.VMEM)
SMEM = pl.BlockSpec(memory_space=pltpu.SMEM)
HBM = pl.BlockSpec(memory_space=pl.ANY)
OFFSETS = ((1, 0), (-1, 0), (1, 1), (-1, 1), (1, -1), (-1, -1), (0, 1), (0, -1))
LAT, LON = 4, 8
WIDE = 512
CHANNELS = 474
CHUNK = 512
ROWS = 2048
NODES = 512
SLOTS = 256
MESH_A, MESH_B = 16, 32


def dot(a, b, ca=1, cb=0):
    return lax.dot_general(a, b, (((ca,), (cb,)), ((), ())), preferred_element_type=F32)


def sigmoid(x):
    return 0.5 * jnp.tanh(0.5 * x) + 0.5


def column(line):
    return jnp.transpose(jnp.broadcast_to(line, (8, line.shape[1])))[:, :1]


def hits(count, codes, dim):
    shape = (codes.shape[0], count) if dim == 1 else (count, codes.shape[1])
    places = lax.broadcasted_iota(jnp.int32, shape, dim)
    return jnp.where(codes.astype(jnp.int32) == places, 1.0, 0.0).astype(BF16)


def halo_rows(step):
    if step[0] != 0 and step[1] != 0:
        return 0
    return MESH_B if step[0] != 0 else MESH_A


def send_kernel(counts_ref, feat_ref, rows_ref, target_ref, cot_ref, mix_ref, *refs):
    outs, (lines, onehot) = refs[: len(OFFSETS)], refs[len(OFFSETS) :]
    lat_index, lon_index = lax.axis_index("lat"), lax.axis_index("lon")
    slots = lax.broadcasted_iota(jnp.int32, (1, SLOTS), 1)
    for k, (di, dj) in enumerate(OFFSETS):
        tile = jnp.clip(lat_index + di, 0, LAT - 1) * LON + lax.rem(lon_index + dj + LON, LON)
        lines[k : k + 1] = rows_ref[pl.ds(tile, 1)].astype(F32)
        code = jnp.where(slots < counts_ref[0, tile], target_ref[pl.ds(tile, 1)] + 1, 0)
        high = lax.shift_right_logical(code, 5)
        lines[8 + k : 9 + k] = high.astype(F32)
        lines[16 + k : 17 + k] = (code - high * 32).astype(F32)
    columns = jnp.transpose(lines[...])
    lane = lax.broadcasted_iota(jnp.int32, (SLOTS, 128), 1)
    for pair in range(0, len(OFFSETS), 2):
        for h in range(2):
            onehot[h * SLOTS : (h + 1) * SLOTS] = hits(ROWS, columns[:, pair + h : pair + h + 1], 1)
        picked = dot(onehot[...], feat_ref[...])
        for h in range(2):
            k = pair + h
            out = outs[k]
            part = picked[h * SLOTS : (h + 1) * SLOTS]
            out[:SLOTS, 384:] = jnp.zeros((SLOTS, 128), BF16)
            out[:SLOTS, :CHANNELS] = part.astype(BF16)
            tail = out[:SLOTS, 384:].astype(F32)
            tail = jnp.where(lane == 90, columns[:, 8 + k : 9 + k], tail)
            tail = jnp.where(lane == 91, columns[:, 16 + k : 17 + k], tail)
            out[:SLOTS, 384:] = tail.astype(BF16)
    mix = mix_ref[...]
    for k, step in enumerate(OFFSETS):
        if halo_rows(step):
            if step[0] != 0:
                edge = cot_ref[MESH_A - 1] if step[0] > 0 else cot_ref[0]
            else:
                edge = cot_ref[:, MESH_B - 1] if step[1] > 0 else cot_ref[:, 0]
            outs[k][SLOTS:] = (mix * edge.astype(F32)).astype(BF16)


def edge_forward(x, codes_col, codes_line, w_grid, w_src, query):
    pre_grid = dot(x, w_grid)
    s = sigmoid(pre_grid)
    latent = (pre_grid * s).astype(BF16)
    slope_grid = (s * (1.0 + pre_grid * (1.0 - s))).astype(BF16)
    pre = dot(latent, w_src) + dot(hits(NODES, codes_col - 1.0, 1), query)
    s = sigmoid(pre)
    message = (pre * s).astype(BF16)
    slope = (s * (1.0 + pre * (1.0 - s))).astype(BF16)
    total = dot(hits(NODES, codes_line - 1.0, 0), message)
    return latent, slope_grid, slope, total


def local_kernel(
    counts_ref, feat_ref, mesh_ref, rows_ref, target_ref, w_grid, w_src, w_dst, bias,
    x_out, latent_out, slope_grid_out, slope_out, total_out, query_out, codes_out,
    w_wide, onehot, query,
):
    w_wide[...] = jnp.zeros((WIDE, WIDE), BF16)
    w_wide[:CHANNELS] = w_grid[...]
    q = dot(mesh_ref[...], w_dst[...]) + bias[...]
    query[...] = q.astype(BF16)
    query_out[...] = query[...]
    total_out[...] = jnp.zeros((NODES, WIDE), F32)
    n = ROWS // CHUNK
    slot = lax.broadcasted_iota(jnp.int32, (1, ROWS), 1)
    codes_out[...] = jnp.where(slot < counts_ref[0], target_ref[...] + 1, 0).astype(F32)

    def step(c, carry):
        at = pl.ds(pl.multiple_of(c * CHUNK, CHUNK), CHUNK)
        onehot[...] = hits(ROWS, column(rows_ref[:, at].astype(F32)), 1)
        x_out[at, 384:] = jnp.zeros((CHUNK, 128), BF16)
        x_out[at, :CHANNELS] = dot(onehot[...], feat_ref[...]).astype(BF16)
        line = codes_out[:, at]
        latent, slope_grid, slope, total = edge_forward(
            x_out[at], column(line), line, w_wide[...], w_src[...], query[...]
        )
        latent_out[at] = latent
        slope_grid_out[at] = slope_grid
        slope_out[at] = slope
        total_out[...] += total
        return carry

    lax.fori_loop(0, n, step, 0)


def main_kernel(
    *refs,
):
    n_in = len(OFFSETS)
    arrived = refs[:n_in]
    (
        x_l, latent_l, slope_grid_l, slope_l, total_l, query_ref, codes_l,
        mesh_ref, cot_ref, w_grid, w_src, w_node, gain, mix,
        grads_out, updated_out, up_out, down_out, left_out, right_out,
        w_wide, x_r, latent_r, slope_grid_r, slope_r, total, codes_r, d_updated, d_agg,
        aggb_s, d_hidden_s, d_query, g_src, g_grid,
    ) = refs[n_in:]
    w_wide[...] = jnp.zeros((WIDE, WIDE), BF16)
    w_wide[:CHANNELS] = w_grid[...]
    for k in range(n_in):
        x_r[k * SLOTS : (k + 1) * SLOTS] = arrived[k][:SLOTS]
    n = ROWS // CHUNK
    total[...] = total_l[...]

    def remote(c, carry):
        at = pl.ds(pl.multiple_of(c * CHUNK, CHUNK), CHUNK)
        x = x_r[at]
        tail = jnp.transpose(x[:, 384:].astype(F32))
        line = tail[90:91] * 32.0 + tail[91:92]
        codes_r[:, at] = line
        latent, slope_grid, slope, add = edge_forward(
            x, column(line), line, w_wide[...], w_src[...], query_ref[...]
        )
        latent_r[at] = latent
        slope_grid_r[at] = slope_grid
        slope_r[at] = slope
        total[...] += add
        return carry

    lax.fori_loop(0, n, remote, 0)

    from_down, from_up = arrived[0], arrived[1]
    from_left, from_right = arrived[6], arrived[7]
    row = lax.broadcasted_iota(jnp.int32, (MESH_B, 1), 0)
    mixed = mix[...]
    gains = gain[...]

    def mixed_at(u):
        return (mixed * cot_ref[u].astype(F32)).astype(BF16).astype(F32)

    def spread(u, carry):
        here = mixed_at(u)
        below = mixed_at(jnp.maximum(u - 1, 0))
        above = mixed_at(jnp.minimum(u + 1, MESH_A - 1))
        below = jnp.where(u > 0, below, from_down[SLOTS:].astype(F32))
        above = jnp.where(u < MESH_A - 1, above, from_up[SLOTS:].astype(F32))
        left = jnp.where(row == 0, pick_row(from_left, u), pltpu.roll(here, 1, 0))
        right = jnp.where(row == MESH_B - 1, pick_row(from_right, u), pltpu.roll(here, MESH_B - 1, 0))
        sums = 0.25 * (above + below + right + left)
        d_updated[pl.ds(pl.multiple_of(u * MESH_B, MESH_B), MESH_B)] = cot_ref[u].astype(F32) + sums
        return carry

    lax.fori_loop(0, MESH_A, spread, 0)

    def node(c, carry):
        at = pl.ds(pl.multiple_of(c * 128, 128), 128)
        aggb = total[at].astype(BF16)
        aggb_s[at] = aggb
        hidden = dot(aggb, w_node[...])
        s = sigmoid(hidden)
        active = hidden * s
        centred = active - jnp.mean(active, axis=-1, keepdims=True)
        scale = lax.rsqrt(jnp.mean(centred * centred, axis=-1, keepdims=True) + LAYER_EPSILON)
        normed = centred * scale
        updated_out[at] = (mesh_ref[at].astype(F32) + normed * gains).astype(BF16)
        q = d_updated[at] * gains
        d_active = scale * (
            q
            - jnp.mean(q, axis=-1, keepdims=True)
            - normed * jnp.mean(q * normed, axis=-1, keepdims=True)
        )
        d_hidden = (d_active * (s * (1.0 + hidden * (1.0 - s)))).astype(BF16)
        d_hidden_s[at] = d_hidden
        d_agg[at] = dot(d_hidden, w_node[...], 1, 1).astype(BF16)
        return carry

    lax.fori_loop(0, NODES // 128, node, 0)
    up_out[...] = updated_out[NODES - MESH_B :]
    down_out[...] = updated_out[:MESH_B]
    wide = updated_out[...].astype(F32).reshape(MESH_A, MESH_B, WIDE)
    left_out[...] = wide[:, 0].astype(BF16)
    right_out[...] = wide[:, MESH_B - 1].astype(BF16)
    d_query[...] = jnp.zeros((NODES, WIDE), F32)
    g_src[...] = jnp.zeros((WIDE, WIDE), F32)
    g_grid[...] = jnp.zeros((WIDE, WIDE), F32)

    def back(x_s, latent_s, slope_grid_s, slope_s, codes_s, c, carry):
        at = pl.ds(pl.multiple_of(c * CHUNK, CHUNK), CHUNK)
        line = codes_s[:, at]
        d_message = dot(hits(NODES, column(line) - 1.0, 1), d_agg[...])
        d_pre = (d_message * slope_s[at].astype(F32)).astype(BF16)
        d_query[...] += dot(hits(NODES, line - 1.0, 0), d_pre)
        g_src[...] += dot(d_pre, latent_s[at], 0, 0)
        d_latent = dot(d_pre, w_src[...], 1, 1)
        d_grid = (d_latent * slope_grid_s[at].astype(F32)).astype(BF16)
        g_grid[...] += dot(d_grid, x_s[at], 0, 0)
        return carry

    lax.fori_loop(0, n, functools.partial(back, x_l, latent_l, slope_grid_l, slope_l, codes_l), 0)
    lax.fori_loop(0, n, functools.partial(back, x_r, latent_r, slope_grid_r, slope_r, codes_r), 0)

    def put(which, value):
        grads_out[:, which] = value.astype(BF16).reshape(32, 16, WIDE)

    put(0, g_grid[...])
    put(1, g_src[...])
    put(2, dot(d_query[...].astype(BF16), mesh_ref[...], 0, 0))
    put(3, dot(d_hidden_s[...], aggb_s[...], 0, 0))


def pick_row(ref, u):
    rows = lax.broadcasted_iota(jnp.int32, (MESH_A, 1), 0)
    return jnp.sum(jnp.where(rows == u, ref[SLOTS:].astype(F32), 0.0), axis=0, keepdims=True)


def final_kernel(
    parts, updated_ref, below_ref, above_ref, left_ref, right_ref, mix,
    mesh_out, g_grid, g_src, g_dst, g_node,
):
    for which, out in enumerate((g_grid, g_src, g_dst, g_node)):
        total = jnp.sum(parts[:, which].astype(F32), axis=0)
        turned = jnp.transpose(total)
        out[...] = turned[: out.shape[0]]
    row = lax.broadcasted_iota(jnp.int32, (MESH_B, 1), 0)
    mixed = mix[...]

    def step(u, carry):
        def line(i):
            return updated_ref[pl.ds(pl.multiple_of(i * MESH_B, MESH_B), MESH_B)].astype(F32)

        def side(ref):
            rows = lax.broadcasted_iota(jnp.int32, (MESH_A, 1), 0)
            return jnp.sum(jnp.where(rows == u, ref[...].astype(F32), 0.0), axis=0, keepdims=True)

        here = line(u)
        below = jnp.where(u > 0, line(jnp.maximum(u - 1, 0)), below_ref[...].astype(F32))
        above = jnp.where(u < MESH_A - 1, line(jnp.minimum(u + 1, MESH_A - 1)), above_ref[...].astype(F32))
        left = jnp.where(row == 0, side(left_ref), pltpu.roll(here, 1, 0))
        right = jnp.where(row == MESH_B - 1, side(right_ref), pltpu.roll(here, MESH_B - 1, 0))
        mesh_out[u] = here + mixed * (0.25 * (above + below + right + left))
        return carry

    lax.fori_loop(0, MESH_A, step, 0)


def shape(*dims, dtype=BF16):
    return jax.ShapeDtypeStruct(dims, dtype)


def route(di, dj):
    return [
        (i * LON + j, (i + di) * LON + (j + dj) % LON)
        for i in range(LAT)
        for j in range(LON)
        if 0 <= i + di < LAT
    ]


def moved(value, step):
    return lax.ppermute(value, ("lat", "lon"), route(*step))


def on_device(
    grid_feat, mesh_in, w_grid, w_src, w_dst, b_edge, w_node, node_gain, mix_gain,
    send_rows, send_target, send_counts, local_rows, local_target, local_counts, cotangent,
):
    feat = grid_feat.reshape(ROWS, CHANNELS)
    mesh = mesh_in.reshape(NODES, WIDE)
    mix = mix_gain.reshape(1, WIDE)
    gain = node_gain.reshape(1, WIDE)
    bias = b_edge.reshape(1, WIDE)
    sends = pl.pallas_call(
        send_kernel,
        out_shape=[shape(SLOTS + halo_rows(s), WIDE) for s in OFFSETS],
        in_specs=[SMEM] + [VMEM] * 5,
        out_specs=[VMEM] * len(OFFSETS),
        scratch_shapes=[pltpu.VMEM((32, SLOTS), F32), pltpu.VMEM((2 * SLOTS, ROWS), BF16)],
        name="send_rows",
        cost_estimate=pl.CostEstimate(flops=4 * 10**9, bytes_accessed=5 * 10**6, transcendentals=0),
    )(send_counts, feat, send_rows[0], send_target[0], cotangent, mix)
    arrived = [moved(value, step) for value, step in zip(sends, OFFSETS)]
    local = pl.pallas_call(
        local_kernel,
        out_shape=[shape(ROWS, WIDE)] * 4
        + [shape(NODES, WIDE, dtype=F32), shape(NODES, WIDE), shape(1, ROWS, dtype=F32)],
        in_specs=[SMEM] + [VMEM] * 8,
        out_specs=[VMEM] * 7,
        scratch_shapes=[
            pltpu.VMEM((WIDE, WIDE), BF16),
            pltpu.VMEM((CHUNK, ROWS), BF16),
            pltpu.VMEM((NODES, WIDE), BF16),
        ],
        name="local_edges",
        cost_estimate=pl.CostEstimate(flops=9 * 10**9, bytes_accessed=14 * 10**6, transcendentals=0),
    )(local_counts, feat, mesh, local_rows, local_target, w_grid, w_src, w_dst, bias)
    big = pltpu.VMEM((ROWS, WIDE), BF16)
    square = pltpu.VMEM((WIDE, WIDE), F32)
    square_b = pltpu.VMEM((WIDE, WIDE), BF16)
    grads, updated, up, down, left, right = pl.pallas_call(
        main_kernel,
        out_shape=[
            shape(32, 4, 16, WIDE), shape(NODES, WIDE), shape(MESH_B, WIDE), shape(MESH_B, WIDE),
            shape(MESH_A, WIDE), shape(MESH_A, WIDE),
        ],
        in_specs=[VMEM] * 22,
        out_specs=[VMEM] * 6,
        scratch_shapes=[
            square_b, big, big, big, big, square, pltpu.VMEM((1, ROWS), F32), square, square_b,
            square_b, square_b, square, square, square,
        ],
        name="nodes_and_back",
        compiler_params=pltpu.CompilerParams(vmem_limit_bytes=60 * 2**20),
        cost_estimate=pl.CostEstimate(flops=16 * 10**9, bytes_accessed=20 * 10**6, transcendentals=0),
    )(*arrived, *local, mesh, cotangent, w_grid, w_src, w_node, gain, mix)
    below = moved(up, (1, 0))
    above = moved(down, (-1, 0))
    on_left = moved(right, (0, 1))
    on_right = moved(left, (0, -1))
    parts = lax.all_to_all(grads.reshape(32, 64, WIDE), ("lat", "lon"), 0, 0, tiled=True)
    return pl.pallas_call(
        final_kernel,
        out_shape=[
            shape(MESH_A, MESH_B, WIDE, dtype=F32), shape(CHANNELS, 16, dtype=F32),
            shape(WIDE, 16, dtype=F32), shape(WIDE, 16, dtype=F32), shape(WIDE, 16, dtype=F32),
        ],
        in_specs=[VMEM] * 7,
        out_specs=[VMEM] * 5,
        name="finish",
    )(parts.reshape(32, 4, 16, WIDE), updated, below, above, on_left, on_right, mix)


def solution(mesh):
    tiles = P(("dp", "lat"), "lon", None)
    lists = ("dp", "lat", "lon")
    return jax.shard_map(
        on_device,
        mesh=mesh,
        in_specs=(
            tiles, tiles, P(), P(), P(), P(), P(), P(), P(),
            P(lists, None, None), P(lists, None, None), P(lists, None),
            P(lists, None), P(lists, None), P(lists), tiles,
        ),
        out_specs=(tiles,) + (P("dp", ("lat", "lon")),) * 4,
        check_vma=False,
    )
```

```python
import functools

import jax
import jax.numpy as jnp
from jax import lax
from jax.experimental import pallas as pl
from jax.experimental.pallas import tpu as pltpu
from jax.sharding import PartitionSpec as P

LAYER_EPSILON = 1e-05
F32 = jnp.float32
BF16 = jnp.bfloat16
VMEM = pl.BlockSpec(memory_space=pltpu.VMEM)
SMEM = pl.BlockSpec(memory_space=pltpu.SMEM)
HBM = pl.BlockSpec(memory_space=pl.ANY)
OFFSETS = ((1, 0), (-1, 0), (1, 1), (-1, 1), (1, -1), (-1, -1), (0, 1), (0, -1))
LAT, LON = 4, 8
WIDE = 512
CHANNELS = 474
CHUNK = 1024
LOCAL_CHUNK = 512
SEND_LIMIT, LOCAL_LIMIT, MAIN_LIMIT = 28, 20, 32
NODE_CHUNK = 128
ROWS = 2048
NODES = 512
SLOTS = 256
MESH_A, MESH_B = 16, 32


def dot(a, b, ca=1, cb=0):
    return lax.dot_general(a, b, (((ca,), (cb,)), ((), ())), preferred_element_type=F32)


def sigmoid(x):
    return 0.5 * jnp.tanh(0.5 * x) + 0.5


def column(line):
    return jnp.transpose(jnp.broadcast_to(line, (8, line.shape[1])))[:, :1]


def hits(count, codes, dim):
    shape = (codes.shape[0], count) if dim == 1 else (count, codes.shape[1])
    places = lax.broadcasted_iota(jnp.int32, shape, dim)
    return jnp.where(codes.astype(jnp.int32) == places, 1.0, 0.0).astype(BF16)


def halo_rows(step):
    if step[0] != 0 and step[1] != 0:
        return 0
    return MESH_B if step[0] != 0 else MESH_A


def send_kernel(counts_ref, feat_ref, rows_ref, target_ref, cot_ref, mix_ref, *refs):
    outs, (flat_out, lines, onehot, spread) = refs[: len(OFFSETS)], refs[len(OFFSETS) :]
    lat_index, lon_index = lax.axis_index("lat"), lax.axis_index("y") * 2 + lax.axis_index("core")
    slots = lax.broadcasted_iota(jnp.int32, (1, SLOTS), 1)
    for k, (di, dj) in enumerate(OFFSETS):
        tile = jnp.clip(lat_index + di, 0, LAT - 1) * LON + lax.rem(lon_index + dj + LON, LON)
        lines[k : k + 1] = rows_ref[pl.ds(tile, 1)].astype(F32)
        code = jnp.where(slots < counts_ref[0, tile], target_ref[pl.ds(tile, 1)] + 1, 0)
        high = lax.shift_right_logical(code, 5)
        lines[8 + k : 9 + k] = high.astype(F32)
        lines[16 + k : 17 + k] = (code - high * 32).astype(F32)
    columns = jnp.transpose(lines[...])
    channels = feat_ref[...].astype(F32)
    for h in range(2):
        spread[h] = channels[:, :, h * 128 : (h + 1) * 128].reshape(CHANNELS * 8, 128)
    flat_out[CHANNELS // 16 * 16 :] = jnp.zeros((WIDE - CHANNELS // 16 * 16, ROWS), BF16)
    for i in range(8):
        for h in range(2):
            at = i * 256 + h * 128
            flat_out[:CHANNELS, at : at + 128] = spread[h, pl.ds(i, CHANNELS, stride=8)].astype(BF16)
    lane = lax.broadcasted_iota(jnp.int32, (SLOTS, 128), 1)
    for pair in range(0, len(OFFSETS), 2):
        for h in range(2):
            onehot[h * SLOTS : (h + 1) * SLOTS] = hits(ROWS, columns[:, pair + h : pair + h + 1], 1)
        picked = dot(onehot[...], flat_out[...], 1, 1)
        for h in range(2):
            k = pair + h
            out = outs[k]
            part = picked[h * SLOTS : (h + 1) * SLOTS]
            out[:SLOTS, :384] = part[:, :384].astype(BF16)
            tail = jnp.where(lane == 90, columns[:, 8 + k : 9 + k], part[:, 384:])
            tail = jnp.where(lane == 91, columns[:, 16 + k : 17 + k], tail)
            out[:SLOTS, 384:] = tail.astype(BF16)
    mix = mix_ref[...]
    for k, step in enumerate(OFFSETS):
        if halo_rows(step):
            if step[0] != 0:
                edge = cot_ref[MESH_A - 1] if step[0] > 0 else cot_ref[0]
            else:
                edge = cot_ref[:, MESH_B - 1] if step[1] > 0 else cot_ref[:, 0]
            outs[k][SLOTS:] = (mix * edge.astype(F32)).astype(BF16)


def edge_forward(x, codes_col, codes_line, w_grid, w_src, query):
    pre_grid = dot(x, w_grid)
    s = sigmoid(pre_grid)
    latent = (pre_grid * s).astype(BF16)
    slope_grid = (s * (1.0 + pre_grid * (1.0 - s))).astype(BF16)
    pre = dot(latent, w_src) + dot(hits(NODES, codes_col - 1.0, 1), query)
    s = sigmoid(pre)
    message = (pre * s).astype(BF16)
    slope = (s * (1.0 + pre * (1.0 - s))).astype(BF16)
    total = dot(hits(NODES, codes_line - 1.0, 0), message)
    return latent, slope_grid, slope, total


def local_kernel(
    counts_ref, feat_ref, mesh_ref, rows_ref, target_ref, w_grid, w_src, w_dst, bias,
    x_out, latent_out, slope_grid_out, slope_out, total_out, query_out,
    w_wide, onehot,
):
    w_wide[...] = jnp.zeros((WIDE, WIDE), BF16)
    w_wide[:CHANNELS] = w_grid[...]
    query_out[...] = (dot(mesh_ref[...], w_dst[...]) + bias[...]).astype(BF16)
    total_out[...] = jnp.zeros((NODES, WIDE), F32)
    slot = lax.broadcasted_iota(jnp.int32, (1, LOCAL_CHUNK), 1)

    def step(c, carry):
        at = pl.ds(pl.multiple_of(c * LOCAL_CHUNK, LOCAL_CHUNK), LOCAL_CHUNK)
        onehot[...] = hits(ROWS, column(rows_ref[:, at].astype(F32)), 1)
        x = dot(onehot[...], feat_ref[...], 1, 1).astype(BF16)
        x_out[at] = x
        line = jnp.where(slot + c * LOCAL_CHUNK < counts_ref[0], target_ref[:, at] + 1, 0).astype(F32)
        latent, slope_grid, slope, total = edge_forward(
            x, column(line), line, w_wide[...], w_src[...], query_out[...]
        )
        latent_out[at] = latent
        slope_grid_out[at] = slope_grid
        slope_out[at] = slope
        total_out[...] += total
        return carry

    lax.fori_loop(0, ROWS // LOCAL_CHUNK, step, 0)


def main_kernel(*refs):
    n_in = len(OFFSETS)
    arrived = refs[:n_in]
    (
        x_l, latent_l, slope_grid_l, slope_l, total_l, query_ref, counts_ref, target_ref,
        mesh_ref, cot_ref, w_grid, w_src, w_node, gain, mix,
        keep_out, send_out, updated_out, up_out, down_out, left_out, right_out,
        w_wide, x_s, latent_s, slope_grid_s, slope_s, total, codes_l, codes_r, d_updated, d_agg,
        aggb_s, d_hidden_s, d_query, g_src, g_grid,
    ) = refs[n_in:]
    w_wide[...] = jnp.zeros((WIDE, WIDE), BF16)
    w_wide[:CHANNELS] = w_grid[...]
    for k in range(n_in):
        x_s[k * SLOTS : (k + 1) * SLOTS] = arrived[k][:SLOTS]
    slot = lax.broadcasted_iota(jnp.int32, (1, ROWS), 1)
    codes_l[...] = jnp.where(slot < counts_ref[0], target_ref[...] + 1, 0).astype(F32)
    total[...] = total_l[...]

    def remote(c, carry):
        at = pl.ds(pl.multiple_of(c * CHUNK, CHUNK), CHUNK)
        x = x_s[at]
        tail = jnp.transpose(x[:, 384:].astype(F32))
        line = tail[90:91] * 32.0 + tail[91:92]
        codes_r[:, at] = line
        latent, slope_grid, slope, add = edge_forward(
            x, column(line), line, w_wide[...], w_src[...], query_ref[...]
        )
        latent_s[at] = latent
        slope_grid_s[at] = slope_grid
        slope_s[at] = slope
        total[...] += add
        return carry

    lax.fori_loop(0, ROWS // CHUNK, remote, 0)

    from_down, from_up = arrived[0], arrived[1]
    from_left, from_right = arrived[6], arrived[7]
    row = lax.broadcasted_iota(jnp.int32, (MESH_B, 1), 0)
    mixed = mix[...]
    gains = gain[...]

    def mixed_at(u):
        return (mixed * cot_ref[u].astype(F32)).astype(BF16).astype(F32)

    def spread(u, carry):
        here = mixed_at(u)
        below = mixed_at(jnp.maximum(u - 1, 0))
        above = mixed_at(jnp.minimum(u + 1, MESH_A - 1))
        below = jnp.where(u > 0, below, from_down[SLOTS:].astype(F32))
        above = jnp.where(u < MESH_A - 1, above, from_up[SLOTS:].astype(F32))
        left = jnp.where(row == 0, pick_row(from_left, u), pltpu.roll(here, 1, 0))
        right = jnp.where(row == MESH_B - 1, pick_row(from_right, u), pltpu.roll(here, MESH_B - 1, 0))
        sums = 0.25 * (above + below + right + left)
        d_updated[pl.ds(pl.multiple_of(u * MESH_B, MESH_B), MESH_B)] = cot_ref[u].astype(F32) + sums
        return carry

    lax.fori_loop(0, MESH_A, spread, 0)

    def node(c, carry):
        at = pl.ds(pl.multiple_of(c * NODE_CHUNK, NODE_CHUNK), NODE_CHUNK)
        aggb = total[at].astype(BF16)
        aggb_s[at] = aggb
        hidden = dot(aggb, w_node[...])
        s = sigmoid(hidden)
        active = hidden * s
        centred = active - jnp.mean(active, axis=-1, keepdims=True)
        scale = lax.rsqrt(jnp.mean(centred * centred, axis=-1, keepdims=True) + LAYER_EPSILON)
        normed = centred * scale
        updated_out[at] = (mesh_ref[at].astype(F32) + normed * gains).astype(BF16)
        q = d_updated[at] * gains
        d_active = scale * (
            q
            - jnp.mean(q, axis=-1, keepdims=True)
            - normed * jnp.mean(q * normed, axis=-1, keepdims=True)
        )
        d_hidden = (d_active * (s * (1.0 + hidden * (1.0 - s)))).astype(BF16)
        d_hidden_s[at] = d_hidden
        d_agg[at] = dot(d_hidden, w_node[...], 1, 1).astype(BF16)
        return carry

    lax.fori_loop(0, NODES // NODE_CHUNK, node, 0)
    up_out[...] = updated_out[NODES - MESH_B :]
    down_out[...] = updated_out[:MESH_B]
    wide = updated_out[...].astype(F32).reshape(MESH_A, MESH_B, WIDE)
    left_out[...] = wide[:, 0].astype(BF16)
    right_out[...] = wide[:, MESH_B - 1].astype(BF16)
    d_query[...] = jnp.zeros((NODES, WIDE), F32)
    g_src[...] = jnp.zeros((WIDE, WIDE), F32)
    g_grid[...] = jnp.zeros((WIDE, WIDE), F32)

    def back(x_s, latent_s, slope_grid_s, slope_s, codes, c, carry):
        at = pl.ds(pl.multiple_of(c * CHUNK, CHUNK), CHUNK)
        line = codes[:, at]
        d_message = dot(hits(NODES, column(line) - 1.0, 1), d_agg[...])
        d_pre = (d_message * slope_s[at].astype(F32)).astype(BF16)
        d_query[...] += dot(hits(NODES, line - 1.0, 0), d_pre)
        g_src[...] += dot(d_pre, latent_s[at], 0, 0)
        d_latent = dot(d_pre, w_src[...], 1, 1)
        d_grid = (d_latent * slope_grid_s[at].astype(F32)).astype(BF16)
        g_grid[...] += dot(d_grid, x_s[at], 0, 0)
        return carry

    for group in (
        (x_l, latent_l, slope_grid_l, slope_l, codes_l),
        (x_s, latent_s, slope_grid_s, slope_s, codes_r),
    ):
        lax.fori_loop(0, ROWS // CHUNK, functools.partial(back, *group), 0)
    mine = lax.axis_index("core")

    def put(which, value):
        parts = value.reshape(16, 2, 16, WIDE)
        first, second = parts[:, 0], parts[:, 1]
        keep_out[:, which] = jnp.where(mine == 0, first, second).astype(BF16)
        send_out[:, which] = jnp.where(mine == 0, second, first).astype(BF16)

    put(0, g_grid[...])
    put(1, g_src[...])
    put(2, dot(d_query[...].astype(BF16), mesh_ref[...], 0, 0))
    put(3, dot(d_hidden_s[...], aggb_s[...], 0, 0))


def pick_row(ref, u):
    rows = lax.broadcasted_iota(jnp.int32, (MESH_A, 1), 0)
    return jnp.sum(jnp.where(rows == u, ref[SLOTS:].astype(F32), 0.0), axis=0, keepdims=True)


def sum_kernel(parts, g_grid, g_src, g_dst, g_node):
    for which, out in enumerate((g_grid, g_src, g_dst, g_node)):
        total = jnp.sum(parts[:, which].astype(F32), axis=0)
        out[...] = total[:, : out.shape[1]]


def mix_kernel(updated_ref, below_ref, above_ref, left_ref, right_ref, mix, mesh_out):
    row = lax.broadcasted_iota(jnp.int32, (MESH_B, 1), 0)
    mixed = mix[...]

    def step(u, carry):
        def line(i):
            return updated_ref[pl.ds(pl.multiple_of(i * MESH_B, MESH_B), MESH_B)].astype(F32)

        def side(ref):
            rows = lax.broadcasted_iota(jnp.int32, (MESH_A, 1), 0)
            return jnp.sum(jnp.where(rows == u, ref[...].astype(F32), 0.0), axis=0, keepdims=True)

        here = line(u)
        below = jnp.where(u > 0, line(jnp.maximum(u - 1, 0)), below_ref[...].astype(F32))
        above = jnp.where(u < MESH_A - 1, line(jnp.minimum(u + 1, MESH_A - 1)), above_ref[...].astype(F32))
        left = jnp.where(row == 0, side(left_ref), pltpu.roll(here, 1, 0))
        right = jnp.where(row == MESH_B - 1, side(right_ref), pltpu.roll(here, MESH_B - 1, 0))
        mesh_out[u] = here + mixed * (0.25 * (above + below + right + left))
        return carry

    lax.fori_loop(0, MESH_A, step, 0)


def shape(*dims, dtype=BF16):
    return jax.ShapeDtypeStruct(dims, dtype)


def route(di, dj):
    return [
        (i * LON + j, (i + di) * LON + (j + dj) % LON)
        for i in range(LAT)
        for j in range(LON)
        if 0 <= i + di < LAT
    ]


def moved(value, step):
    return lax.ppermute(value, ("lat", "y", "core"), route(*step))


def cost(flops, bytes_accessed):
    return pl.CostEstimate(flops=flops, bytes_accessed=bytes_accessed, transcendentals=0)


def call_send(counts, feat, rows, target, cotangent, mix):
    return pl.pallas_call(
        send_kernel,
        out_shape=[shape(SLOTS + halo_rows(s), WIDE) for s in OFFSETS] + [shape(WIDE, ROWS)],
        in_specs=[SMEM] + [VMEM] * 5,
        out_specs=[VMEM] * (len(OFFSETS) + 1),
        scratch_shapes=[
            pltpu.VMEM((32, SLOTS), F32),
            pltpu.VMEM((2 * SLOTS, ROWS), BF16),
            pltpu.VMEM((2, CHANNELS * 8, 128), F32),
        ],
        name="send_rows",
        compiler_params=pltpu.CompilerParams(vmem_limit_bytes=SEND_LIMIT * 2**20),
        cost_estimate=cost(5 * 10**9, 6 * 10**6),
    )(counts, feat, rows, target, cotangent, mix)


def call_local(counts, feat, mesh, rows, target, w_grid, w_src, w_dst, bias):
    return pl.pallas_call(
        local_kernel,
        out_shape=[shape(ROWS, WIDE)] * 4 + [shape(NODES, WIDE, dtype=F32), shape(NODES, WIDE)],
        in_specs=[SMEM] + [VMEM] * 8,
        out_specs=[VMEM] * 6,
        scratch_shapes=[pltpu.VMEM((WIDE, WIDE), BF16), pltpu.VMEM((LOCAL_CHUNK, ROWS), BF16)],
        name="local_edges",
        compiler_params=pltpu.CompilerParams(vmem_limit_bytes=LOCAL_LIMIT * 2**20),
        cost_estimate=cost(9 * 10**9, 14 * 10**6),
    )(counts, feat, mesh, rows, target, w_grid, w_src, w_dst, bias)


def call_main(arrived, local, counts, target, mesh, cotangent, w_grid, w_src, w_node, gain, mix):
    big = pltpu.VMEM((ROWS, WIDE), BF16)
    square = pltpu.VMEM((WIDE, WIDE), F32)
    square_b = pltpu.VMEM((WIDE, WIDE), BF16)
    line = pltpu.VMEM((1, ROWS), F32)
    return pl.pallas_call(
        main_kernel,
        out_shape=[shape(16, 4, 16, WIDE)] * 2
        + [shape(NODES, WIDE), shape(MESH_B, WIDE), shape(MESH_B, WIDE)]
        + [shape(MESH_A, WIDE), shape(MESH_A, WIDE)],
        in_specs=[VMEM] * 14 + [SMEM] + [VMEM] * 8,
        out_specs=[VMEM] * 7,
        scratch_shapes=[
            square_b, big, big, big, big, square, line, line, square, square_b,
            square_b, square_b, square, square, square,
        ],
        name="nodes_and_back",
        compiler_params=pltpu.CompilerParams(vmem_limit_bytes=MAIN_LIMIT * 2**20),
        cost_estimate=cost(16 * 10**9, 20 * 10**6),
    )(*arrived, *local, counts, target, mesh, cotangent, w_grid, w_src, w_node, gain, mix)


def call_mix(updated, below, above, left, right, mix):
    return pl.pallas_call(
        mix_kernel,
        out_shape=shape(MESH_A, MESH_B, WIDE, dtype=F32),
        in_specs=[VMEM] * 6,
        out_specs=VMEM,
        name="mix",
        compiler_params=pltpu.CompilerParams(vmem_limit_bytes=8 * 2**20),
        cost_estimate=cost(10**7, 2 * 10**6),
    )(updated, below, above, left, right, mix)


def call_sum(parts):
    return pl.pallas_call(
        sum_kernel,
        out_shape=[shape(16, CHANNELS, dtype=F32)] + [shape(16, WIDE, dtype=F32)] * 3,
        in_specs=[VMEM],
        out_specs=[VMEM] * 4,
        name="sum_parts",
        compiler_params=pltpu.CompilerParams(vmem_limit_bytes=8 * 2**20),
    )(parts)


def on_device(
    grid_feat, mesh_in, w_grid, w_src, w_dst, b_edge, w_node, node_gain, mix_gain,
    send_rows, send_target, send_counts, local_rows, local_target, local_counts, cotangent,
):
    feat = jnp.transpose(grid_feat, (2, 0, 1))
    mesh = mesh_in.reshape(NODES, WIDE)
    mix = mix_gain.reshape(1, WIDE)
    gain = node_gain.reshape(1, WIDE)
    bias = b_edge.reshape(1, WIDE)
    *sends, flat = call_send(send_counts, feat, send_rows[0], send_target[0], cotangent, mix)
    arrived = [moved(value, step) for value, step in zip(sends, OFFSETS)]
    local = call_local(local_counts, flat, mesh, local_rows, local_target, w_grid, w_src, w_dst, bias)
    keep, send, updated, up, down, left, right = call_main(
        arrived, local, local_counts, local_target, mesh, cotangent, w_grid, w_src, w_node, gain, mix
    )
    got = lax.ppermute(send, ("core",), [(0, 1), (1, 0)])
    below = moved(up, (1, 0))
    above = moved(down, (-1, 0))
    on_left = moved(right, (0, 1))
    on_right = moved(left, (0, -1))
    both = (keep.astype(F32) + got.astype(F32)).astype(BF16)
    parts = lax.all_to_all(both.reshape(16, 64, WIDE), ("lat", "y"), 0, 0, tiled=True)
    mesh_out = call_mix(updated, below, above, on_left, on_right, mix)
    sums = call_sum(parts.reshape(16, 4, 16, WIDE))
    return (mesh_out,) + tuple(g.T for g in sums)


def solution(mesh):
    fine = jax.sharding.Mesh(mesh.devices.reshape(4, LAT, LON // 2, 2), ("dp", "lat", "y", "core"))
    lists = ("dp", "lat", "y", "core")
    tiles = P(("dp", "lat"), ("y", "core"), None)
    return jax.shard_map(
        on_device,
        mesh=fine,
        in_specs=(
            tiles, tiles, P(), P(), P(), P(), P(), P(), P(),
            P(lists, None, None), P(lists, None, None), P(lists, None),
            P(lists, None), P(lists, None), P(lists), tiles,
        ),
        out_specs=(tiles,) + (P("dp", ("lat", "y", "core")),) * 4,
        check_vma=False,
    )
```

```python
import functools

import jax
import jax.numpy as jnp
from jax import lax
from jax.experimental import pallas as pl
from jax.experimental.pallas import tpu as pltpu
from jax.sharding import PartitionSpec as P

LAYER_EPSILON = 1e-05
F32 = jnp.float32
BF16 = jnp.bfloat16
VMEM = pl.BlockSpec(memory_space=pltpu.VMEM)
SMEM = pl.BlockSpec(memory_space=pltpu.SMEM)
HBM = pl.BlockSpec(memory_space=pl.ANY)
SWAPS = ((1, 1), (2, 1), (1, 2), (2, 2), (1, 0), (2, 0), (0, 1), (0, 2))
LAT, LON = 4, 8
PEERS = LAT * LON
WIDE = 512
CHANNELS = 474
CHUNK = 1024
CHUNK_R = 1280
LOCAL_CHUNK = 1024
SEND_LIMIT, LOCAL_LIMIT, MAIN_LIMIT = 36 * 2**20, 28, 34
NODE_CHUNK = 128
ROWS = 2048
NODES = 512
SLOTS = 256
MESH_A, MESH_B = 16, 32


def dot(a, b, ca=1, cb=0):
    return lax.dot_general(a, b, (((ca,), (cb,)), ((), ())), preferred_element_type=F32)


def sigmoid(x):
    return 0.5 * jnp.tanh(0.5 * x) + 0.5


def column(line):
    return jnp.transpose(jnp.broadcast_to(line, (8, line.shape[1])))[:, :1]


def hits(count, codes, dim):
    shape = (codes.shape[0], count) if dim == 1 else (count, codes.shape[1])
    places = lax.broadcasted_iota(jnp.int32, shape, dim)
    return jnp.where(codes.astype(jnp.int32) == places, 1.0, 0.0).astype(BF16)


def toward(kind, index):
    odd = lax.rem(index, 2)
    return (0, 1 - 2 * odd, 2 * odd - 1)[kind]


def halo_rows(swap):
    return 0 if swap[0] and swap[1] else (MESH_B if swap[0] else MESH_A)


def send_kernel(counts_hbm, feat_hbm, rows_hbm, target_hbm, cot_hbm, mix_hbm, *refs):
    n = len(SWAPS)
    results, flat_result, outs, rest = refs[:n], refs[n], refs[n + 1 : 2 * n + 1], refs[2 * n + 1 :]
    (
        flat_out, lines, onehot, spread, counts_ref, feat_ref, rows_ref, target_ref, cot_ref, mix_ref,
        sems, out_sems,
    ) = rest
    fetches = [
        pltpu.make_async_copy(src, dst, sems.at[k])
        for k, (src, dst) in enumerate(
            (
                (feat_hbm, feat_ref), (counts_hbm, counts_ref), (rows_hbm, rows_ref),
                (target_hbm, target_ref), (cot_hbm, cot_ref), (mix_hbm, mix_ref),
            )
        )
    ]
    for fetch in fetches:
        fetch.start()
    lat_index, lon_index = lax.axis_index("lat"), lax.axis_index("y") * 2 + lax.axis_index("core")
    slots = lax.broadcasted_iota(jnp.int32, (1, SLOTS), 1)
    flat_out[CHANNELS // 16 * 16 :] = jnp.zeros((WIDE - CHANNELS // 16 * 16, ROWS), BF16)
    for fetch in fetches[1:4]:
        fetch.wait()
    tiles = []
    for k, (i, j) in enumerate(SWAPS):
        di, dj = toward(i, lat_index), toward(j, lon_index)
        tile = jnp.clip(lat_index + di, 0, LAT - 1) * LON + lax.rem(lon_index + dj + LON, LON)
        tiles.append(tile)
        lines[k : k + 1] = rows_ref[pl.ds(tile, 1)].astype(F32)
        code = jnp.where(slots < counts_ref[0, tile], target_ref[pl.ds(tile, 1)] + 1, 0)
        high = lax.shift_right_logical(code, 5)
        lines[8 + k : 9 + k] = high.astype(F32)
        lines[16 + k : 17 + k] = (code - high * 32).astype(F32)
    for fetch in fetches[:1] + fetches[4:]:
        fetch.wait()
    columns = jnp.transpose(lines[...])
    channels = feat_ref[...].astype(F32)
    for h in range(2):
        spread[h] = channels[:, :, h * 128 : (h + 1) * 128].reshape(CHANNELS * 8, 128)
    flat_out[CHANNELS // 16 * 16 :] = jnp.zeros((WIDE - CHANNELS // 16 * 16, ROWS), BF16)
    for i in range(8):
        for h in range(2):
            at = i * 256 + h * 128
            flat_out[:CHANNELS, at : at + 128] = spread[h, pl.ds(i, CHANNELS, stride=8)].astype(BF16)
    stores = [pltpu.make_async_copy(flat_out, flat_result, out_sems.at[n])]
    stores[0].start()
    mix = mix_ref[...]
    for k, (i, j) in enumerate(SWAPS):
        if halo_rows((i, j)) == MESH_B:
            edge = cot_ref[jnp.where(toward(i, lat_index) > 0, MESH_A - 1, 0)]
        elif halo_rows((i, j)) == MESH_A:
            edge = jnp.where(
                toward(j, lon_index) > 0,
                cot_ref[:, MESH_B - 1].astype(F32),
                cot_ref[:, 0].astype(F32),
            )
        else:
            continue
        outs[k][SLOTS:] = (mix * edge.astype(F32)).astype(BF16)
    lane = lax.broadcasted_iota(jnp.int32, (SLOTS, 128), 1)
    for pair in range(0, len(SWAPS), 2):
        for h in range(2):
            onehot[h * SLOTS : (h + 1) * SLOTS] = hits(ROWS, columns[:, pair + h : pair + h + 1], 1)
        picked = dot(onehot[...], flat_out[...], 1, 1)
        for h in range(2):
            k = pair + h
            out = outs[k]
            part = picked[h * SLOTS : (h + 1) * SLOTS]
            out[:SLOTS, :384] = part[:, :384].astype(BF16)
            tail = jnp.where(lane == 90, columns[:, 8 + k : 9 + k], part[:, 384:])
            tail = jnp.where(lane == 91, columns[:, 16 + k : 17 + k], tail)
            tail = jnp.where(lane == 92, counts_ref[0, tiles[k]].astype(F32), tail)
            out[:SLOTS, 384:] = tail.astype(BF16)
            stores.append(pltpu.make_async_copy(out, results[k], out_sems.at[k]))
            stores[-1].start()
    for store in stores:
        store.wait()


def silu_parts(half):
    t = jnp.tanh(half)
    up, down = 1.0 + t, 1.0 - t
    return half * up, up * (1.0 + half * down)


def edge_forward(x, codes_col, codes_line, w_grid, w_src, query):
    active, slope_grid = silu_parts(dot(x, w_grid))
    latent = active.astype(BF16)
    active, slope = silu_parts(dot(latent, w_src) + dot(hits(NODES, codes_col - 1.0, 1), query))
    total = dot(hits(NODES, codes_line - 1.0, 0), active.astype(BF16))
    return latent, slope_grid.astype(BF16), slope.astype(BF16), total


def halve(out, weights):
    rows = weights.shape[0]
    if rows < WIDE:
        out[...] = jnp.zeros((WIDE, WIDE), BF16)
    out[:rows] = (0.5 * weights[...].astype(F32)).astype(BF16)


def local_kernel(
    counts_ref, feat_ref, mesh_ref, rows_ref, target_ref, w_grid, w_src, w_dst, bias,
    x_out, latent_out, slope_grid_out, slope_out, total_out, query_out, w_wide, w_half,
    onehot,
):
    halve(w_wide, w_grid)
    halve(w_half, w_src)
    query_out[...] = (0.5 * (dot(mesh_ref[...], w_dst[...]) + bias[...])).astype(BF16)
    total_out[...] = jnp.zeros((NODES, WIDE), F32)
    slot = lax.broadcasted_iota(jnp.int32, (1, LOCAL_CHUNK), 1)

    def step(c, carry):
        at = pl.ds(pl.multiple_of(c * LOCAL_CHUNK, LOCAL_CHUNK), LOCAL_CHUNK)
        onehot[...] = hits(ROWS, column(rows_ref[:, at].astype(F32)), 1)
        x = dot(onehot[...], feat_ref[...], 1, 1).astype(BF16)
        x_out[at] = x
        line = jnp.where(slot + c * LOCAL_CHUNK < counts_ref[0], target_ref[:, at] + 1, 0).astype(F32)
        latent, slope_grid, slope, total = edge_forward(
            x, column(line), line, w_wide[...], w_half[...], query_out[...]
        )
        latent_out[at] = latent
        slope_grid_out[at] = slope_grid
        slope_out[at] = slope
        total_out[...] += total
        return carry

    lax.fori_loop(0, ROWS // LOCAL_CHUNK, step, 0)


def main_kernel(*refs):
    n_in = len(SWAPS)
    arrived = refs[:n_in]
    (
        x_l, latent_l, slope_grid_l, slope_l, total_l, query_ref, w_wide, w_half, counts_ref, target_ref,
        mesh_ref, cot_ref, w_node, gain, mix,
        keep_out, send_out, updated_out, row_1, row_2, column_1, column_2,
        x_s, latent_s, slope_grid_s, slope_s, total, codes_l, codes_r, d_updated, d_agg,
        aggb_s, d_hidden_s, d_query, g_src, g_grid, padded,
    ) = refs[n_in:]
    lane = lax.broadcasted_iota(jnp.int32, (16, 128), 1)
    filled = 0
    for k in range(n_in):
        x_s[pl.ds(pl.multiple_of(filled, 16), SLOTS)] = arrived[k][:SLOTS]
        first = jnp.where(lane == 92, arrived[k][:16, 384:].astype(F32), 0.0)
        filled += lax.shift_right_logical(jnp.max(first).astype(jnp.int32) + 15, 4) * 16
    x_s[pl.ds(pl.multiple_of(filled, 16), CHUNK_R)] = jnp.zeros((CHUNK_R, WIDE), BF16)
    chunks = lax.div(filled + CHUNK_R - 1, CHUNK_R)
    slot = lax.broadcasted_iota(jnp.int32, (1, ROWS), 1)
    codes_l[...] = jnp.where(slot < counts_ref[0], target_ref[...] + 1, 0).astype(F32)
    total[...] = total_l[...]

    def remote(c, carry):
        at = pl.ds(pl.multiple_of(c * CHUNK_R, CHUNK_R), CHUNK_R)
        x = x_s[at]
        tail = jnp.transpose(x[:, 384:].astype(F32))
        line = tail[90:91] * 32.0 + tail[91:92]
        codes_r[:, at] = line
        latent, slope_grid, slope, add = edge_forward(
            x, column(line), line, w_wide[...], w_half[...], query_ref[...]
        )
        latent_s[at] = latent
        slope_grid_s[at] = slope_grid
        slope_s[at] = slope
        total[...] += add
        return carry

    lax.fori_loop(0, chunks, remote, 0)

    lat_odd, mine = lax.rem(lax.axis_index("lat"), 2), lax.axis_index("core")
    from_down, from_up = swapped(lat_odd, arrived[4][SLOTS:], arrived[5][SLOTS:])
    from_left, from_right = swapped(mine, arrived[6][SLOTS:], arrived[7][SLOTS:])
    row = lax.broadcasted_iota(jnp.int32, (MESH_B, 1), 0)
    mixed = mix[...]
    gains = gain[...]

    padded[0] = from_down
    padded[MESH_A + 1] = from_up

    def blend(u, carry):
        padded[u + 1] = (mixed * cot_ref[u].astype(F32)).astype(BF16).astype(F32)
        return carry

    lax.fori_loop(0, MESH_A, blend, 0)

    def spread(u, carry):
        here = padded[u + 1]
        left = jnp.where(row == 0, pick_row(from_left, u), pltpu.roll(here, 1, 0))
        right = jnp.where(row == MESH_B - 1, pick_row(from_right, u), pltpu.roll(here, MESH_B - 1, 0))
        sums = 0.25 * (padded[u + 2] + padded[u] + right + left)
        d_updated[pl.ds(pl.multiple_of(u * MESH_B, MESH_B), MESH_B)] = cot_ref[u].astype(F32) + sums
        return carry

    lax.fori_loop(0, MESH_A, spread, 0)

    def node(c, carry):
        at = pl.ds(pl.multiple_of(c * NODE_CHUNK, NODE_CHUNK), NODE_CHUNK)
        aggb = total[at].astype(BF16)
        aggb_s[at] = aggb
        hidden = dot(aggb, w_node[...])
        s = sigmoid(hidden)
        active = hidden * s
        centred = active - jnp.mean(active, axis=-1, keepdims=True)
        scale = lax.rsqrt(jnp.mean(centred * centred, axis=-1, keepdims=True) + LAYER_EPSILON)
        normed = centred * scale
        updated_out[at] = (mesh_ref[at].astype(F32) + normed * gains).astype(BF16)
        q = d_updated[at] * gains
        d_active = scale * (
            q
            - jnp.mean(q, axis=-1, keepdims=True)
            - normed * jnp.mean(q * normed, axis=-1, keepdims=True)
        )
        d_hidden = (d_active * (s * (1.0 + hidden * (1.0 - s)))).astype(BF16)
        d_hidden_s[at] = d_hidden
        d_agg[at] = (0.5 * dot(d_hidden, w_node[...], 1, 1)).astype(BF16)
        return carry

    lax.fori_loop(0, NODES // NODE_CHUNK, node, 0)
    rows = swapped(lat_odd, updated_out[:MESH_B], updated_out[NODES - MESH_B :])
    wide = updated_out[...].astype(F32).reshape(MESH_A, MESH_B, WIDE)
    columns = swapped(mine, wide[:, 0], wide[:, MESH_B - 1])
    for out, value in zip((row_1, row_2, column_1, column_2), rows + columns):
        out[...] = value.astype(BF16)
    d_query[...] = jnp.zeros((NODES, WIDE), F32)
    g_src[...] = jnp.zeros((WIDE, WIDE), F32)
    g_grid[...] = jnp.zeros((WIDE, WIDE), F32)

    def back(x_s, latent_s, slope_grid_s, slope_s, codes, size, c, carry):
        at = pl.ds(pl.multiple_of(c * size, size), size)
        line = codes[:, at]
        d_message = dot(hits(NODES, column(line) - 1.0, 1), d_agg[...])
        d_pre = (d_message * slope_s[at].astype(F32)).astype(BF16)
        d_query[...] += dot(hits(NODES, line - 1.0, 0), d_pre)
        g_src[...] += dot(d_pre, latent_s[at], 0, 0)
        d_latent = dot(d_pre, w_half[...], 1, 1)
        d_grid = (d_latent * slope_grid_s[at].astype(F32)).astype(BF16)
        g_grid[...] += dot(d_grid, x_s[at], 0, 0)
        return carry

    mine_s = (x_l, latent_l, slope_grid_l, slope_l, codes_l, CHUNK)
    theirs = (x_s, latent_s, slope_grid_s, slope_s, codes_r, CHUNK_R)
    lax.fori_loop(0, ROWS // CHUNK, functools.partial(back, *mine_s), 0)
    lax.fori_loop(0, chunks, functools.partial(back, *theirs), 0)

    def put(which, value):
        parts = value.reshape(16, 2, 16, WIDE)
        first, second = parts[:, 0], parts[:, 1]
        keep_out[:, which] = jnp.where(mine == 0, first, second).astype(BF16)
        send_out[:, which] = jnp.where(mine == 0, second, first).astype(BF16)

    put(0, g_grid[...])
    put(1, g_src[...])
    put(2, dot(d_query[...].astype(BF16), mesh_ref[...], 0, 0))
    put(3, dot(d_hidden_s[...], aggb_s[...], 0, 0))


def swapped(odd, first, second):
    first, second = first.astype(F32), second.astype(F32)
    return jnp.where(odd == 1, first, second), jnp.where(odd == 1, second, first)


def pick_row(rows, u):
    places = lax.broadcasted_iota(jnp.int32, (MESH_A, 1), 0)
    return jnp.sum(jnp.where(places == u, rows, 0.0), axis=0, keepdims=True)


def sum_kernel(parts, g_grid, g_src, g_dst, g_node):
    for which, out in enumerate((g_grid, g_src, g_dst, g_node)):
        total = jnp.sum(parts[:, which].astype(F32), axis=0)
        out[...] = total[:, : out.shape[1]]


def mix_kernel(updated_ref, row_1, row_2, column_1, column_2, mix, mesh_out):
    from_down, from_up = swapped(lax.rem(lax.axis_index("lat"), 2), row_1[...], row_2[...])
    from_left, from_right = swapped(lax.axis_index("core"), column_1[...], column_2[...])
    row = lax.broadcasted_iota(jnp.int32, (MESH_B, 1), 0)
    mixed = mix[...]

    def step(u, carry):
        def line(i):
            return updated_ref[pl.ds(pl.multiple_of(i * MESH_B, MESH_B), MESH_B)].astype(F32)

        here = line(u)
        below = jnp.where(u > 0, line(jnp.maximum(u - 1, 0)), from_down)
        above = jnp.where(u < MESH_A - 1, line(jnp.minimum(u + 1, MESH_A - 1)), from_up)
        left = jnp.where(row == 0, pick_row(from_left, u), pltpu.roll(here, 1, 0))
        right = jnp.where(row == MESH_B - 1, pick_row(from_right, u), pltpu.roll(here, MESH_B - 1, 0))
        mesh_out[u] = here + mixed * (0.25 * (above + below + right + left))
        return carry

    lax.fori_loop(0, MESH_A, step, 0)


def shape(*dims, dtype=BF16):
    return jax.ShapeDtypeStruct(dims, dtype)


def route(i, j):
    def step(kind, index):
        odd = index % 2
        return index + (0, 1 - 2 * odd, 2 * odd - 1)[kind]

    return [
        (a * LON + b, step(i, a) * LON + step(j, b) % LON)
        for a in range(LAT)
        for b in range(LON)
        if 0 <= step(i, a) < LAT
    ]


def moved(value, swap):
    return lax.ppermute(value, ("lat", "y", "core"), route(*swap))


def cost(flops, bytes_accessed):
    return pl.CostEstimate(flops=flops, bytes_accessed=bytes_accessed, transcendentals=0)


def call_send(counts, feat, rows, target, cotangent, mix):
    return pl.pallas_call(
        send_kernel,
        out_shape=[shape(SLOTS + halo_rows(s), WIDE) for s in SWAPS] + [shape(WIDE, ROWS)],
        in_specs=[pl.BlockSpec(memory_space=pltpu.HBM)] * 6,
        out_specs=[HBM] * (len(SWAPS) + 1),
        scratch_shapes=[pltpu.VMEM((SLOTS + halo_rows(s), WIDE), BF16) for s in SWAPS]
        + [
            pltpu.VMEM((WIDE, ROWS), BF16),
            pltpu.VMEM((32, SLOTS), F32),
            pltpu.VMEM((2 * SLOTS, ROWS), BF16),
            pltpu.VMEM((2, CHANNELS * 8, 128), F32),
            pltpu.SMEM((1, PEERS), jnp.int32),
            pltpu.VMEM((CHANNELS, 8, 256), BF16),
            pltpu.VMEM((PEERS, SLOTS), jnp.int32),
            pltpu.VMEM((PEERS, SLOTS), jnp.int32),
            pltpu.VMEM((MESH_A, MESH_B, WIDE), BF16),
            pltpu.VMEM((1, WIDE), F32),
            pltpu.SemaphoreType.DMA((6,)),
            pltpu.SemaphoreType.DMA((len(SWAPS) + 1,)),
        ],
        name="send_rows",
        compiler_params=pltpu.CompilerParams(vmem_limit_bytes=SEND_LIMIT),
        cost_estimate=cost(5 * 10**9, 6 * 10**6),
    )(counts, feat, rows, target, cotangent, mix)


def call_local(counts, feat, mesh, rows, target, w_grid, w_src, w_dst, bias):
    return pl.pallas_call(
        local_kernel,
        out_shape=[shape(ROWS, WIDE)] * 4 + [shape(NODES, WIDE, dtype=F32)] + [shape(NODES, WIDE)] * 3,
        in_specs=[SMEM] + [VMEM] * 8,
        out_specs=[VMEM] * 8,
        scratch_shapes=[pltpu.VMEM((LOCAL_CHUNK, ROWS), BF16)],
        name="local_edges",
        compiler_params=pltpu.CompilerParams(vmem_limit_bytes=LOCAL_LIMIT * 2**20),
        cost_estimate=cost(9 * 10**9, 14 * 10**6),
    )(counts, feat, mesh, rows, target, w_grid, w_src, w_dst, bias)


def call_main(arrived, local, counts, target, mesh, cotangent, w_node, gain, mix):
    big = pltpu.VMEM((2 * CHUNK_R, WIDE), BF16)
    square = pltpu.VMEM((WIDE, WIDE), F32)
    square_b = pltpu.VMEM((WIDE, WIDE), BF16)
    line = pltpu.VMEM((1, ROWS), F32)
    line_r = pltpu.VMEM((1, 2 * CHUNK_R), F32)
    return pl.pallas_call(
        main_kernel,
        out_shape=[shape(16, 4, 16, WIDE)] * 2
        + [shape(NODES, WIDE), shape(MESH_B, WIDE), shape(MESH_B, WIDE)]
        + [shape(MESH_A, WIDE), shape(MESH_A, WIDE)],
        in_specs=[VMEM] * 16 + [SMEM] + [VMEM] * 6,
        out_specs=[VMEM] * 7,
        scratch_shapes=[
            pltpu.VMEM((ROWS + CHUNK_R, WIDE), BF16), big, big, big, square,
            line, line_r, square, square_b,
            square_b, square_b, square, square, square, pltpu.VMEM((MESH_A + 2, MESH_B, WIDE), F32),
        ],
        name="nodes_and_back",
        compiler_params=pltpu.CompilerParams(vmem_limit_bytes=MAIN_LIMIT * 2**20),
        cost_estimate=cost(16 * 10**9, 20 * 10**6),
    )(*arrived, *local, counts, target, mesh, cotangent, w_node, gain, mix)


def call_mix(updated, row_1, row_2, column_1, column_2, mix):
    return pl.pallas_call(
        mix_kernel,
        out_shape=shape(MESH_A, MESH_B, WIDE, dtype=F32),
        in_specs=[VMEM] * 6,
        out_specs=VMEM,
        name="mix",
        compiler_params=pltpu.CompilerParams(vmem_limit_bytes=8 * 2**20),
        cost_estimate=cost(10**7, 2 * 10**6),
    )(updated, row_1, row_2, column_1, column_2, mix)


def call_sum(parts):
    return pl.pallas_call(
        sum_kernel,
        out_shape=[shape(16, CHANNELS, dtype=F32)] + [shape(16, WIDE, dtype=F32)] * 3,
        in_specs=[VMEM],
        out_specs=[VMEM] * 4,
        name="sum_parts",
        compiler_params=pltpu.CompilerParams(vmem_limit_bytes=8 * 2**20),
    )(parts)


def on_device(
    grid_feat, mesh_in, w_grid, w_src, w_dst, b_edge, w_node, node_gain, mix_gain,
    send_rows, send_target, send_counts, local_rows, local_target, local_counts, cotangent,
):
    feat = pltpu.with_memory_space_constraint(jnp.transpose(grid_feat, (2, 0, 1)), pltpu.HBM)
    mesh = mesh_in.reshape(NODES, WIDE)
    mix = mix_gain.reshape(1, WIDE)
    gain = node_gain.reshape(1, WIDE)
    bias = b_edge.reshape(1, WIDE)
    held = [pltpu.with_memory_space_constraint(v, pltpu.HBM) for v in (send_counts, send_rows[0], send_target[0], cotangent, mix)]
    *sends, flat = call_send(held[0], feat, *held[1:])
    arrived = [moved(value, step) for value, step in zip(sends, SWAPS)]
    local = call_local(local_counts, flat, mesh, local_rows, local_target, w_grid, w_src, w_dst, bias)
    keep, send, updated, *halos = call_main(
        arrived, local, local_counts, local_target, mesh, cotangent, w_node, gain, mix
    )
    got = lax.ppermute(send, ("core",), [(0, 1), (1, 0)])
    halos = [moved(v, swap) for v, swap in zip(halos, ((1, 0), (2, 0), (0, 1), (0, 2)))]
    both = (keep.astype(F32) + got.astype(F32)).astype(BF16)
    parts = lax.all_to_all(both.reshape(16, 64, WIDE), ("lat", "y"), 0, 0, tiled=True)
    mesh_out = call_mix(updated, *halos, mix)
    sums = call_sum(parts.reshape(16, 4, 16, WIDE))
    return (mesh_out,) + tuple(g.T for g in sums)


def solution(mesh):
    fine = jax.sharding.Mesh(mesh.devices.reshape(4, LAT, LON // 2, 2), ("dp", "lat", "y", "core"))
    lists = ("dp", "lat", "y", "core")
    tiles = P(("dp", "lat"), ("y", "core"), None)
    return jax.shard_map(
        on_device,
        mesh=fine,
        in_specs=(
            tiles, tiles, P(), P(), P(), P(), P(), P(), P(),
            P(lists, None, None), P(lists, None, None), P(lists, None),
            P(lists, None), P(lists, None), P(lists), tiles,
        ),
        out_specs=(tiles,) + (P("dp", ("lat", "y", "core")),) * 4,
        check_vma=False,
    )
```

```python
import functools

import jax
import jax.numpy as jnp
from jax import lax
from jax.experimental import pallas as pl
from jax.experimental.pallas import tpu as pltpu
from jax.sharding import PartitionSpec as P

LAYER_EPSILON = 1e-05
F32 = jnp.float32
BF16 = jnp.bfloat16
VMEM = pl.BlockSpec(memory_space=pltpu.VMEM)
SMEM = pl.BlockSpec(memory_space=pltpu.SMEM)
HBM = pl.BlockSpec(memory_space=pl.ANY)
SWAPS = ((1, 1), (2, 1), (1, 2), (2, 2), (1, 0), (2, 0), (0, 1), (0, 2))
LAT, LON = 4, 8
PEERS = LAT * LON
WIDE = 512
CHANNELS = 474
CHUNK = 1024
CHUNK_R = 1280
GROUP = 4
LOCAL_CHUNK = 1024
SEND_LIMIT, LOCAL_LIMIT, MAIN_LIMIT = 36 * 2**20, 28, 34
NODE_CHUNK = 256
ROWS = 2048
NODES = 512
SLOTS = 256
MESH_A, MESH_B = 16, 32


def dot(a, b, ca=1, cb=0):
    return lax.dot_general(a, b, (((ca,), (cb,)), ((), ())), preferred_element_type=F32)


def sigmoid(x):
    return 0.5 * jnp.tanh(0.5 * x) + 0.5


def column(line):
    return jnp.transpose(jnp.broadcast_to(line, (8, line.shape[1])))[:, :1]


def hits(count, codes, dim):
    shape = (codes.shape[0], count) if dim == 1 else (count, codes.shape[1])
    places = lax.broadcasted_iota(jnp.int32, shape, dim)
    return jnp.where(codes.astype(jnp.int32) == places, 1.0, 0.0).astype(BF16)


def toward(kind, index):
    odd = lax.rem(index, 2)
    return (0, 1 - 2 * odd, 2 * odd - 1)[kind]


def halo_rows(swap):
    return 0 if swap[0] and swap[1] else (MESH_B if swap[0] else MESH_A)


def send_kernel(counts_hbm, feat_hbm, rows_hbm, target_hbm, cot_hbm, mix_hbm, *refs):
    n = len(SWAPS)
    kept_hbm, refs = refs[:4], refs[4:]
    results, flat_out, kept, rest = refs[:n], refs[n], refs[n + 1 : n + 5], refs[n + 5 :]
    (
        packed, row_halo, column_halo, lines, spread, counts_ref, feat_ref, rows_ref, target_ref,
        cot_ref, mix_ref, sems, out_sems,
    ) = rest
    cuts = list(range(0, CHANNELS, 128)) + [CHANNELS]
    parts = list(zip(cuts[:-1], cuts[1:]))
    feat_fetches = [
        pltpu.make_async_copy(feat_hbm.at[lo:hi], feat_ref.at[lo:hi], sems.at[5 + k])
        for k, (lo, hi) in enumerate(parts)
    ]
    fetches = [
        pltpu.make_async_copy(src, dst, sems.at[k])
        for k, (src, dst) in enumerate(
            (
                (counts_hbm, counts_ref), (rows_hbm, rows_ref), (target_hbm, target_ref),
                (cot_hbm, cot_ref), (mix_hbm, mix_ref),
            )
        )
    ]
    keeps = [pltpu.make_async_copy(src, dst, sems.at[9 + k]) for k, (src, dst) in enumerate(zip(kept_hbm, kept))]
    for fetch in fetches[:3] + feat_fetches + fetches[3:] + keeps:
        fetch.start()
    lat_index, lon_index = lax.axis_index("lat"), lax.axis_index("y") * 2 + lax.axis_index("core")
    slots = lax.broadcasted_iota(jnp.int32, (1, SLOTS), 1)
    flat_out[CHANNELS // 16 * 16 :] = jnp.zeros((WIDE - CHANNELS // 16 * 16, ROWS), BF16)
    for fetch in fetches[:3]:
        fetch.wait()
    for k, (i, j) in enumerate(SWAPS):
        di, dj = toward(i, lat_index), toward(j, lon_index)
        tile = jnp.clip(lat_index + di, 0, LAT - 1) * LON + lax.rem(lon_index + dj + LON, LON)
        count = counts_ref[0, tile]
        lines[k : k + 1] = rows_ref[pl.ds(tile, 1)].astype(F32)
        code = jnp.where(slots < count, target_ref[pl.ds(tile, 1)] + 1, 0)
        high = lax.shift_right_logical(code, 5)
        lines[8 + k : 9 + k] = high.astype(F32)
        lines[16 + k : 17 + k] = (code - high * 32).astype(F32)
        lines[24 + k : 25 + k] = jnp.zeros((1, SLOTS), F32) + count.astype(F32)
    for fetch, (lo, hi) in zip(feat_fetches, parts):
        fetch.wait()
        channels = feat_ref[lo:hi].astype(F32)
        for h in range(2):
            spread[h, : (hi - lo) * 8] = channels[:, :, h * 128 : (h + 1) * 128].reshape((hi - lo) * 8, 128)
        for i in range(8):
            for h in range(2):
                at = i * 256 + h * 128
                flat_out[lo:hi, at : at + 128] = spread[h, pl.ds(i, hi - lo, stride=8)].astype(BF16)
    lane = lax.broadcasted_iota(jnp.int32, (SLOTS, 128), 1)

    def gather(p, carry):
        picks = [column(lines[pl.ds(p * GROUP + h, 1)]) for h in range(GROUP)]
        picked = dot(hits(ROWS, jnp.concatenate(picks, axis=0), 1), flat_out[...], 1, 1)
        for h in range(GROUP):
            k = p * GROUP + h
            part = picked[h * SLOTS : (h + 1) * SLOTS]
            packed[k, :, :384] = part[:, :384].astype(BF16)
            tail = part[:, 384:]
            for place in range(3):
                extra = column(lines[pl.ds(8 * (place + 1) + k, 1)])
                tail = jnp.where(lane == 90 + place, extra, tail)
            packed[k, :, 384:] = tail.astype(BF16)
        return carry

    lax.fori_loop(0, n // GROUP, gather, 0)
    stores = [
        pltpu.make_async_copy(packed.at[k], result.at[pl.ds(0, SLOTS)], out_sems.at[k])
        for k, result in enumerate(results)
    ]
    for store in stores:
        store.start()
    for fetch in fetches[3:]:
        fetch.wait()
    mix = mix_ref[...]
    for k, (i, j) in enumerate(SWAPS):
        size = halo_rows((i, j))
        if size == MESH_B:
            edge = cot_ref[jnp.where(toward(i, lat_index) > 0, MESH_A - 1, 0)]
            buffer = row_halo
        elif size == MESH_A:
            edge = jnp.where(
                toward(j, lon_index) > 0,
                cot_ref[:, MESH_B - 1].astype(F32),
                cot_ref[:, 0].astype(F32),
            )
            buffer = column_halo
        else:
            continue
        buffer[k % 2] = (mix * edge.astype(F32)).astype(BF16)
        stores.append(
            pltpu.make_async_copy(buffer.at[k % 2], results[k].at[pl.ds(SLOTS, size)], out_sems.at[4 + k])
        )
        stores[-1].start()
    for store in stores + keeps:
        store.wait()


def silu_parts(half):
    t = jnp.tanh(half)
    up, down = 1.0 + t, 1.0 - t
    return half * up, up * (1.0 + half * down)


def edge_forward(x, codes_col, codes_line, w_grid, w_src, query):
    active, slope_grid = silu_parts(dot(x, w_grid))
    latent = active.astype(BF16)
    active, slope = silu_parts(dot(latent, w_src) + dot(hits(NODES, codes_col - 1.0, 1), query))
    total = dot(hits(NODES, codes_line - 1.0, 0), active.astype(BF16))
    return latent, slope_grid.astype(BF16), slope.astype(BF16), total


def halve(out, weights):
    rows = weights.shape[0]
    if rows < WIDE:
        out[...] = jnp.zeros((WIDE, WIDE), BF16)
    out[:rows] = (0.5 * weights[...].astype(F32)).astype(BF16)


def local_kernel(
    counts_ref, feat_ref, rows_ref, target_ref, bias, mesh_ref, w_grid, w_src, w_dst,
    x_out, latent_out, slope_grid_out, slope_out, total_out, query_out, w_wide, w_half,
):
    total_out[...] = jnp.zeros((NODES, WIDE), F32)
    halve(w_wide, w_grid)
    halve(w_half, w_src)
    query_out[...] = (0.5 * (dot(mesh_ref[...], w_dst[...]) + bias[...])).astype(BF16)
    slot = lax.broadcasted_iota(jnp.int32, (1, LOCAL_CHUNK), 1)

    def step(c, carry):
        at = pl.ds(pl.multiple_of(c * LOCAL_CHUNK, LOCAL_CHUNK), LOCAL_CHUNK)
        picks = hits(ROWS, column(rows_ref[:, at].astype(F32)), 1)
        x = dot(picks, feat_ref[...], 1, 1).astype(BF16)
        x_out[at] = x
        line = jnp.where(slot + c * LOCAL_CHUNK < counts_ref[0], target_ref[:, at] + 1, 0).astype(F32)
        latent, slope_grid, slope, total = edge_forward(
            x, column(line), line, w_wide[...], w_half[...], query_out[...]
        )
        latent_out[at] = latent
        slope_grid_out[at] = slope_grid
        slope_out[at] = slope
        total_out[...] += total
        return carry

    lax.fori_loop(0, ROWS // LOCAL_CHUNK, step, 0)


def main_kernel(*refs):
    n_in = len(SWAPS)
    arrived = refs[:n_in]
    (
        x_l, latent_l, slope_grid_l, slope_l, total_l, query_ref, w_wide, w_half, counts_ref, target_ref,
        mesh_ref, cot_ref, w_node, gain, mix,
        keep_out, send_out, updated_out, row_1, row_2, column_1, column_2,
        x_s, latent_s, slope_grid_s, slope_s, total, codes_l, codes_r, d_updated, d_agg,
        aggb_s, d_hidden_s, d_query, g_src, g_grid, padded,
    ) = refs[n_in:]
    lane = lax.broadcasted_iota(jnp.int32, (16, 128), 1)
    filled = 0
    for k in range(n_in):
        x_s[pl.ds(pl.multiple_of(filled, 16), SLOTS)] = arrived[k][:SLOTS]
        first = jnp.where(lane == 92, arrived[k][:16, 384:].astype(F32), 0.0)
        filled += lax.shift_right_logical(jnp.max(first).astype(jnp.int32) + 15, 4) * 16
    x_s[pl.ds(pl.multiple_of(filled, 16), CHUNK_R)] = jnp.zeros((CHUNK_R, WIDE), BF16)
    chunks = lax.div(filled + CHUNK_R - 1, CHUNK_R)
    slot = lax.broadcasted_iota(jnp.int32, (1, ROWS), 1)
    codes_l[...] = jnp.where(slot < counts_ref[0], target_ref[...] + 1, 0).astype(F32)
    total[...] = total_l[...]

    def remote(c, carry):
        at = pl.ds(pl.multiple_of(c * CHUNK_R, CHUNK_R), CHUNK_R)
        x = x_s[at]
        tail = jnp.transpose(x[:, 384:].astype(F32))
        line = tail[90:91] * 32.0 + tail[91:92]
        codes_r[:, at] = line
        latent, slope_grid, slope, add = edge_forward(
            x, column(line), line, w_wide[...], w_half[...], query_ref[...]
        )
        latent_s[at] = latent
        slope_grid_s[at] = slope_grid
        slope_s[at] = slope
        total[...] += add
        return carry

    lax.fori_loop(0, chunks, remote, 0)

    lat_odd, mine = lax.rem(lax.axis_index("lat"), 2), lax.axis_index("core")
    from_down, from_up = swapped(lat_odd, arrived[4][SLOTS:], arrived[5][SLOTS:])
    from_left, from_right = swapped(mine, arrived[6][SLOTS:], arrived[7][SLOTS:])
    row = lax.broadcasted_iota(jnp.int32, (MESH_B, 1), 0)
    mixed = mix[...]
    gains = gain[...]

    padded[0] = from_down
    padded[MESH_A + 1] = from_up

    def blend(u, carry):
        padded[u + 1] = (mixed * cot_ref[u].astype(F32)).astype(BF16).astype(F32)
        return carry

    lax.fori_loop(0, MESH_A, blend, 0)

    def spread(u, carry):
        here = padded[u + 1]
        left = jnp.where(row == 0, pick_row(from_left, u), pltpu.roll(here, 1, 0))
        right = jnp.where(row == MESH_B - 1, pick_row(from_right, u), pltpu.roll(here, MESH_B - 1, 0))
        sums = 0.25 * (padded[u + 2] + padded[u] + right + left)
        d_updated[pl.ds(pl.multiple_of(u * MESH_B, MESH_B), MESH_B)] = cot_ref[u].astype(F32) + sums
        return carry

    lax.fori_loop(0, MESH_A, spread, 0)

    def node(c, carry):
        at = pl.ds(pl.multiple_of(c * NODE_CHUNK, NODE_CHUNK), NODE_CHUNK)
        aggb = total[at].astype(BF16)
        aggb_s[at] = aggb
        hidden = dot(aggb, w_node[...])
        s = sigmoid(hidden)
        active = hidden * s
        centred = active - jnp.mean(active, axis=-1, keepdims=True)
        scale = lax.rsqrt(jnp.mean(centred * centred, axis=-1, keepdims=True) + LAYER_EPSILON)
        normed = centred * scale
        updated_out[at] = (mesh_ref[at].astype(F32) + normed * gains).astype(BF16)
        q = d_updated[at] * gains
        d_active = scale * (
            q
            - jnp.mean(q, axis=-1, keepdims=True)
            - normed * jnp.mean(q * normed, axis=-1, keepdims=True)
        )
        d_hidden = (d_active * (s * (1.0 + hidden * (1.0 - s)))).astype(BF16)
        d_hidden_s[at] = d_hidden
        d_agg[at] = (0.5 * dot(d_hidden, w_node[...], 1, 1)).astype(BF16)
        return carry

    lax.fori_loop(0, NODES // NODE_CHUNK, node, 0)
    rows = swapped(lat_odd, updated_out[:MESH_B], updated_out[NODES - MESH_B :])
    wide = updated_out[...].astype(F32).reshape(MESH_A, MESH_B, WIDE)
    columns = swapped(mine, wide[:, 0], wide[:, MESH_B - 1])
    for out, value in zip((row_1, row_2, column_1, column_2), rows + columns):
        out[...] = value.astype(BF16)
    d_query[...] = jnp.zeros((NODES, WIDE), F32)
    g_src[...] = jnp.zeros((WIDE, WIDE), F32)
    g_grid[...] = jnp.zeros((WIDE, WIDE), F32)

    def back(x_s, latent_s, slope_grid_s, slope_s, codes, size, c, carry):
        at = pl.ds(pl.multiple_of(c * size, size), size)
        line = codes[:, at]
        d_message = dot(hits(NODES, column(line) - 1.0, 1), d_agg[...])
        d_pre = (d_message * slope_s[at].astype(F32)).astype(BF16)
        d_query[...] += dot(hits(NODES, line - 1.0, 0), d_pre)
        g_src[...] += dot(d_pre, latent_s[at], 0, 0)
        d_latent = dot(d_pre, w_half[...], 1, 1)
        d_grid = (d_latent * slope_grid_s[at].astype(F32)).astype(BF16)
        g_grid[...] += dot(d_grid, x_s[at], 0, 0)
        return carry

    mine_s = (x_l, latent_l, slope_grid_l, slope_l, codes_l, CHUNK)
    theirs = (x_s, latent_s, slope_grid_s, slope_s, codes_r, CHUNK_R)
    lax.fori_loop(0, ROWS // CHUNK, functools.partial(back, *mine_s), 0)
    lax.fori_loop(0, chunks, functools.partial(back, *theirs), 0)

    def put(which, value):
        parts = value.reshape(16, 2, 16, WIDE)
        first, second = parts[:, 0], parts[:, 1]
        keep_out[:, which] = jnp.where(mine == 0, first, second).astype(BF16)
        send_out[:, which] = jnp.where(mine == 0, second, first).astype(BF16)

    put(0, g_grid[...])
    put(1, g_src[...])
    put(2, dot(d_query[...].astype(BF16), mesh_ref[...], 0, 0))
    put(3, dot(d_hidden_s[...], aggb_s[...], 0, 0))


def swapped(odd, first, second):
    first, second = first.astype(F32), second.astype(F32)
    return jnp.where(odd == 1, first, second), jnp.where(odd == 1, second, first)


def pick_row(rows, u):
    places = lax.broadcasted_iota(jnp.int32, (MESH_A, 1), 0)
    return jnp.sum(jnp.where(places == u, rows, 0.0), axis=0, keepdims=True)


def finish_kernel(
    parts, updated_ref, row_1, row_2, column_1, column_2, mix,
    mesh_out, g_grid, g_src, g_dst, g_node, mesh_s, sem,
):
    from_down, from_up = swapped(lax.rem(lax.axis_index("lat"), 2), row_1[...], row_2[...])
    from_left, from_right = swapped(lax.axis_index("core"), column_1[...], column_2[...])
    row = lax.broadcasted_iota(jnp.int32, (MESH_B, 1), 0)
    mixed = mix[...]

    def step(u, carry):
        def line(i):
            return updated_ref[pl.ds(pl.multiple_of(i * MESH_B, MESH_B), MESH_B)].astype(F32)

        here = line(u)
        below = jnp.where(u > 0, line(jnp.maximum(u - 1, 0)), from_down)
        above = jnp.where(u < MESH_A - 1, line(jnp.minimum(u + 1, MESH_A - 1)), from_up)
        left = jnp.where(row == 0, pick_row(from_left, u), pltpu.roll(here, 1, 0))
        right = jnp.where(row == MESH_B - 1, pick_row(from_right, u), pltpu.roll(here, MESH_B - 1, 0))
        mesh_s[u] = here + mixed * (0.25 * (above + below + right + left))
        return carry

    lax.fori_loop(0, MESH_A, step, 0)
    store = pltpu.make_async_copy(mesh_s, mesh_out, sem)
    store.start()
    for which, out in enumerate((g_grid, g_src, g_dst, g_node)):
        total = jnp.sum(parts[:, which].astype(F32), axis=0)
        out[...] = total[:, : out.shape[1]]
    store.wait()


def shape(*dims, dtype=BF16):
    return jax.ShapeDtypeStruct(dims, dtype)


def route(i, j):
    def step(kind, index):
        odd = index % 2
        return index + (0, 1 - 2 * odd, 2 * odd - 1)[kind]

    return [
        (a * LON + b, step(i, a) * LON + step(j, b) % LON)
        for a in range(LAT)
        for b in range(LON)
        if 0 <= step(i, a) < LAT
    ]


def moved(value, swap):
    return lax.ppermute(value, ("lat", "y", "core"), route(*swap))


def in_hbm(value):
    return pltpu.with_memory_space_constraint(value, pltpu.HBM)


def cost(flops, bytes_accessed):
    return pl.CostEstimate(flops=flops, bytes_accessed=bytes_accessed, transcendentals=0)


def call_send(*operands):
    return pl.pallas_call(
        send_kernel,
        out_shape=[shape(SLOTS + halo_rows(s), WIDE) for s in SWAPS]
        + [shape(WIDE, ROWS)]
        + [shape(*v.shape) for v in operands[6:]],
        in_specs=[pl.BlockSpec(memory_space=pltpu.HBM)] * 10,
        out_specs=[HBM] * len(SWAPS) + [VMEM] * 5,
        scratch_shapes=[
            pltpu.VMEM((len(SWAPS), SLOTS, WIDE), BF16),
            pltpu.VMEM((2, MESH_B, WIDE), BF16),
            pltpu.VMEM((2, MESH_A, WIDE), BF16),
            pltpu.VMEM((32, SLOTS), F32),
            pltpu.VMEM((2, 128 * 8, 128), F32),
            pltpu.SMEM((1, PEERS), jnp.int32),
            pltpu.VMEM((CHANNELS, 8, 256), BF16),
            pltpu.VMEM((PEERS, SLOTS), jnp.int32),
            pltpu.VMEM((PEERS, SLOTS), jnp.int32),
            pltpu.VMEM((MESH_A, MESH_B, WIDE), BF16),
            pltpu.VMEM((1, WIDE), F32),
            pltpu.SemaphoreType.DMA((13,)),
            pltpu.SemaphoreType.DMA((12,)),
        ],
        name="send_rows",
        compiler_params=pltpu.CompilerParams(vmem_limit_bytes=SEND_LIMIT),
        cost_estimate=cost(5 * 10**9, 6 * 10**6),
    )(*(in_hbm(v) for v in operands))


def call_local(counts, feat, rows, target, bias, mesh, w_grid, w_src, w_dst):
    return pl.pallas_call(
        local_kernel,
        out_shape=[shape(ROWS, WIDE)] * 4 + [shape(NODES, WIDE, dtype=F32)] + [shape(NODES, WIDE)] * 3,
        in_specs=[SMEM] + [VMEM] * 8,
        out_specs=[VMEM] * 8,
        name="local_edges",
        compiler_params=pltpu.CompilerParams(vmem_limit_bytes=LOCAL_LIMIT * 2**20),
        cost_estimate=cost(9 * 10**9, 14 * 10**6),
    )(counts, feat, rows, target, bias, mesh, w_grid, w_src, w_dst)


def call_main(arrived, local, counts, target, mesh, cotangent, w_node, gain, mix):
    big = pltpu.VMEM((2 * CHUNK_R, WIDE), BF16)
    square = pltpu.VMEM((WIDE, WIDE), F32)
    square_b = pltpu.VMEM((WIDE, WIDE), BF16)
    line = pltpu.VMEM((1, ROWS), F32)
    line_r = pltpu.VMEM((1, 2 * CHUNK_R), F32)
    return pl.pallas_call(
        main_kernel,
        out_shape=[shape(16, 4, 16, WIDE)] * 2
        + [shape(NODES, WIDE), shape(MESH_B, WIDE), shape(MESH_B, WIDE)]
        + [shape(MESH_A, WIDE), shape(MESH_A, WIDE)],
        in_specs=[VMEM] * 16 + [SMEM] + [VMEM] * 6,
        out_specs=[VMEM] * 7,
        scratch_shapes=[
            pltpu.VMEM((ROWS + CHUNK_R, WIDE), BF16), big, big, big, square,
            line, line_r, square, square_b,
            square_b, square_b, square, square, square, pltpu.VMEM((MESH_A + 2, MESH_B, WIDE), F32),
        ],
        name="nodes_and_back",
        compiler_params=pltpu.CompilerParams(vmem_limit_bytes=MAIN_LIMIT * 2**20),
        cost_estimate=cost(16 * 10**9, 20 * 10**6),
    )(*arrived, *local, counts, target, mesh, cotangent, w_node, gain, mix)


def call_finish(parts, updated, row_1, row_2, column_1, column_2, mix):
    return pl.pallas_call(
        finish_kernel,
        out_shape=[shape(MESH_A, MESH_B, WIDE, dtype=F32), shape(16, CHANNELS, dtype=F32)]
        + [shape(16, WIDE, dtype=F32)] * 3,
        in_specs=[VMEM] * 7,
        out_specs=[HBM] + [VMEM] * 4,
        scratch_shapes=[pltpu.VMEM((MESH_A, MESH_B, WIDE), F32), pltpu.SemaphoreType.DMA],
        name="finish",
        compiler_params=pltpu.CompilerParams(vmem_limit_bytes=8 * 2**20),
    )(parts, updated, row_1, row_2, column_1, column_2, mix)


def on_device(
    grid_feat, mesh_in, w_grid, w_src, w_dst, b_edge, w_node, node_gain, mix_gain,
    send_rows, send_target, send_counts, local_rows, local_target, local_counts, cotangent,
):
    feat = jnp.transpose(grid_feat, (2, 0, 1))
    mesh = mesh_in.reshape(NODES, WIDE)
    mix = mix_gain.reshape(1, WIDE)
    gain = node_gain.reshape(1, WIDE)
    bias = b_edge.reshape(1, WIDE)
    *sends, flat, mesh_v, w_grid, w_src, w_dst = call_send(
        send_counts, feat, send_rows[0], send_target[0], cotangent, mix, mesh, w_grid, w_src, w_dst
    )
    arrived = [moved(value, step) for value, step in zip(sends, SWAPS)]
    local = call_local(local_counts, flat, local_rows, local_target, bias, mesh_v, w_grid, w_src, w_dst)
    keep, send, updated, *halos = call_main(
        arrived, local, local_counts, local_target, mesh, cotangent, w_node, gain, mix
    )
    got = lax.ppermute(send, ("core",), [(0, 1), (1, 0)])
    halos = [moved(v, swap) for v, swap in zip(halos, ((1, 0), (2, 0), (0, 1), (0, 2)))]
    both = (keep.astype(F32) + got.astype(F32)).astype(BF16)
    parts = lax.all_to_all(both.reshape(16, 64, WIDE), ("lat", "y"), 0, 0, tiled=True)
    mesh_out, *sums = call_finish(parts.reshape(16, 4, 16, WIDE), updated, *halos, mix)
    return (mesh_out,) + tuple(g.T for g in sums)


def solution(mesh):
    fine = jax.sharding.Mesh(mesh.devices.reshape(4, LAT, LON // 2, 2), ("dp", "lat", "y", "core"))
    lists = ("dp", "lat", "y", "core")
    tiles = P(("dp", "lat"), ("y", "core"), None)
    return jax.shard_map(
        on_device,
        mesh=fine,
        in_specs=(
            tiles, tiles, P(), P(), P(), P(), P(), P(), P(),
            P(lists, None, None), P(lists, None, None), P(lists, None),
            P(lists, None), P(lists, None), P(lists), tiles,
        ),
        out_specs=(tiles,) + (P("dp", ("lat", "y", "core")),) * 4,
        check_vma=False,
    )
```

```python
import functools

import jax
import jax.numpy as jnp
from jax import lax
from jax.experimental import pallas as pl
from jax.experimental.pallas import tpu as pltpu
from jax.sharding import PartitionSpec as P

LAYER_EPSILON = 1e-05
F32 = jnp.float32
BF16 = jnp.bfloat16
VMEM = pl.BlockSpec(memory_space=pltpu.VMEM)
SMEM = pl.BlockSpec(memory_space=pltpu.SMEM)
HBM = pl.BlockSpec(memory_space=pl.ANY)
SWAPS = ((1, 1), (2, 1), (1, 2), (2, 2), (1, 0), (2, 0), (0, 1), (0, 2))
LAT, LON = 4, 8
PEERS = LAT * LON
WIDE = 512
CHANNELS = 474
CHUNK = 1024
CHUNK_R = 1280
CHUNK_S = 640
LOCAL_CHUNK = 1024
SEND_LIMIT, LOCAL_LIMIT, MAIN_LIMIT = 36 * 2**20, 28, 34
NODE_CHUNK = 256
ROWS = 2048
NODES = 512
SLOTS = 256
MESH_A, MESH_B = 16, 32


def dot(a, b, ca=1, cb=0):
    return lax.dot_general(a, b, (((ca,), (cb,)), ((), ())), preferred_element_type=F32)


def sigmoid(x):
    return 0.5 * jnp.tanh(0.5 * x) + 0.5


def column(line):
    return jnp.transpose(jnp.broadcast_to(line, (8, line.shape[1])))[:, :1]


def hits(count, codes, dim):
    shape = (codes.shape[0], count) if dim == 1 else (count, codes.shape[1])
    places = lax.broadcasted_iota(jnp.int32, shape, dim)
    return jnp.where(codes.astype(jnp.int32) == places, 1.0, 0.0).astype(BF16)


def toward(kind, index):
    odd = lax.rem(index, 2)
    return (0, 1 - 2 * odd, 2 * odd - 1)[kind]


def halo_rows(swap):
    return 0 if swap[0] and swap[1] else (MESH_B if swap[0] else MESH_A)


def send_kernel(counts_hbm, feat_hbm, rows_hbm, target_hbm, cot_hbm, mix_hbm, *refs):
    n = len(SWAPS)
    kept_hbm, refs = refs[:4], refs[4:]
    results, flat_out, kept, rest = refs[:n], refs[n], refs[n + 1 : n + 5], refs[n + 5 :]
    (
        packed, row_halo, column_halo, lines, spread, counts_ref, feat_ref, rows_ref, target_ref,
        cot_ref, mix_ref, sems, out_sems,
    ) = rest
    cuts = list(range(0, CHANNELS, 128)) + [CHANNELS]
    parts = list(zip(cuts[:-1], cuts[1:]))
    feat_fetches = [
        pltpu.make_async_copy(feat_hbm.at[lo:hi], feat_ref.at[lo:hi], sems.at[5 + k])
        for k, (lo, hi) in enumerate(parts)
    ]
    fetches = [
        pltpu.make_async_copy(src, dst, sems.at[k])
        for k, (src, dst) in enumerate(
            (
                (counts_hbm, counts_ref), (rows_hbm, rows_ref), (target_hbm, target_ref),
                (cot_hbm, cot_ref), (mix_hbm, mix_ref),
            )
        )
    ]
    keeps = [pltpu.make_async_copy(src, dst, sems.at[9 + k]) for k, (src, dst) in enumerate(zip(kept_hbm, kept))]
    for fetch in fetches[:3] + feat_fetches + fetches[3:] + keeps:
        fetch.start()
    lat_index, lon_index = lax.axis_index("lat"), lax.axis_index("y") * 2 + lax.axis_index("core")
    slots = lax.broadcasted_iota(jnp.int32, (1, SLOTS), 1)
    flat_out[CHANNELS // 16 * 16 :] = jnp.zeros((WIDE - CHANNELS // 16 * 16, ROWS), BF16)
    for fetch in fetches[:3]:
        fetch.wait()
    lines[...] = jnp.zeros(lines.shape, F32)
    starts, filled = [], 0
    for i, j in SWAPS:
        di, dj = toward(i, lat_index), toward(j, lon_index)
        there = (lat_index + di >= 0) & (lat_index + di < LAT)
        tile = jnp.clip(lat_index + di, 0, LAT - 1) * LON + lax.rem(lon_index + dj + LON, LON)
        count = counts_ref[0, tile]
        at = pl.ds(pl.multiple_of(filled, 128), SLOTS)
        code = jnp.where(slots < count, target_ref[pl.ds(tile, 1)] + 1, 0)
        high = lax.shift_right_logical(code, 5)
        lines[0:1, at] = rows_ref[pl.ds(tile, 1)].astype(F32)
        lines[1:2, at] = high.astype(F32)
        lines[2:3, at] = (code - high * 32).astype(F32)
        lines[3:4, at] = jnp.zeros((1, SLOTS), F32) + count.astype(F32)
        starts.append(filled)
        filled += jnp.where(there, jnp.where(count > 128, 256, 128), 0)
    for fetch, (lo, hi) in zip(feat_fetches, parts):
        fetch.wait()
        channels = feat_ref[lo:hi].astype(F32)
        for h in range(2):
            spread[h, : (hi - lo) * 8] = channels[:, :, h * 128 : (h + 1) * 128].reshape((hi - lo) * 8, 128)
        for i in range(8):
            for h in range(2):
                at = i * 256 + h * 128
                flat_out[lo:hi, at : at + 128] = spread[h, pl.ds(i, hi - lo, stride=8)].astype(BF16)
    lane = lax.broadcasted_iota(jnp.int32, (CHUNK_S, 128), 1)

    def gather(p, carry):
        at = pl.ds(pl.multiple_of(p * CHUNK_S, CHUNK_S), CHUNK_S)
        picked = dot(hits(ROWS, column(lines[0:1, at]), 1), flat_out[...], 1, 1)
        packed[at, :384] = picked[:, :384].astype(BF16)
        tail = picked[:, 384:]
        for place in range(3):
            tail = jnp.where(lane == 90 + place, column(lines[place + 1 : place + 2, at]), tail)
        packed[at, 384:] = tail.astype(BF16)
        return carry

    lax.fori_loop(0, lax.div(filled + CHUNK_S - 1, CHUNK_S), gather, 0)
    stores = [
        pltpu.make_async_copy(
            packed.at[pl.ds(pl.multiple_of(starts[k], 128), SLOTS)], result.at[pl.ds(0, SLOTS)], out_sems.at[k]
        )
        for k, result in enumerate(results)
    ]
    for store in stores:
        store.start()
    for fetch in fetches[3:]:
        fetch.wait()
    mix = mix_ref[...]
    for k, (i, j) in enumerate(SWAPS):
        size = halo_rows((i, j))
        if size == MESH_B:
            edge = cot_ref[jnp.where(toward(i, lat_index) > 0, MESH_A - 1, 0)]
            buffer = row_halo
        elif size == MESH_A:
            edge = jnp.where(
                toward(j, lon_index) > 0,
                cot_ref[:, MESH_B - 1].astype(F32),
                cot_ref[:, 0].astype(F32),
            )
            buffer = column_halo
        else:
            continue
        buffer[k % 2] = (mix * edge.astype(F32)).astype(BF16)
        stores.append(
            pltpu.make_async_copy(buffer.at[k % 2], results[k].at[pl.ds(SLOTS, size)], out_sems.at[4 + k])
        )
        stores[-1].start()
    for store in stores + keeps:
        store.wait()


def silu_parts(half):
    t = jnp.tanh(half)
    up, down = 1.0 + t, 1.0 - t
    return half * up, up * (1.0 + half * down)


def edge_forward(x, codes_col, codes_line, w_grid, w_src, query):
    active, slope_grid = silu_parts(dot(x, w_grid))
    latent = active.astype(BF16)
    active, slope = silu_parts(dot(latent, w_src) + dot(hits(NODES, codes_col - 1.0, 1), query))
    total = dot(hits(NODES, codes_line - 1.0, 0), active.astype(BF16))
    return latent, slope_grid.astype(BF16), slope.astype(BF16), total


def halve(out, weights):
    rows = weights.shape[0]
    if rows < WIDE:
        out[...] = jnp.zeros((WIDE, WIDE), BF16)
    out[:rows] = (0.5 * weights[...].astype(F32)).astype(BF16)


def local_kernel(
    counts_ref, feat_ref, rows_ref, target_ref, bias, mesh_ref, w_grid, w_src, w_dst,
    x_out, latent_out, slope_grid_out, slope_out, total_out, query_out, w_wide, w_half,
):
    total_out[...] = jnp.zeros((NODES, WIDE), F32)
    halve(w_wide, w_grid)
    halve(w_half, w_src)
    query_out[...] = (0.5 * (dot(mesh_ref[...], w_dst[...]) + bias[...])).astype(BF16)
    slot = lax.broadcasted_iota(jnp.int32, (1, LOCAL_CHUNK), 1)

    def step(c, carry):
        at = pl.ds(pl.multiple_of(c * LOCAL_CHUNK, LOCAL_CHUNK), LOCAL_CHUNK)
        picks = hits(ROWS, column(rows_ref[:, at].astype(F32)), 1)
        x = dot(picks, feat_ref[...], 1, 1).astype(BF16)
        x_out[at] = x
        line = jnp.where(slot + c * LOCAL_CHUNK < counts_ref[0], target_ref[:, at] + 1, 0).astype(F32)
        latent, slope_grid, slope, total = edge_forward(
            x, column(line), line, w_wide[...], w_half[...], query_out[...]
        )
        latent_out[at] = latent
        slope_grid_out[at] = slope_grid
        slope_out[at] = slope
        total_out[...] += total
        return carry

    lax.fori_loop(0, ROWS // LOCAL_CHUNK, step, 0)


def main_kernel(*refs):
    n_in = len(SWAPS)
    arrived = refs[:n_in]
    (
        x_l, latent_l, slope_grid_l, slope_l, total_l, query_ref, w_wide, w_half, counts_ref, target_ref,
        mesh_ref, cot_ref, w_node, gain, mix,
        keep_out, send_out, updated_out, row_1, row_2, column_1, column_2,
        x_s, latent_s, slope_grid_s, slope_s, total, codes_l, codes_r, d_updated, d_agg,
        aggb_s, d_hidden_s, d_query, g_src, g_grid, padded, sides,
    ) = refs[n_in:]
    lane = lax.broadcasted_iota(jnp.int32, (16, 128), 1)
    filled = 0
    for k in range(n_in):
        x_s[pl.ds(pl.multiple_of(filled, 16), SLOTS)] = arrived[k][:SLOTS]
        first = jnp.where(lane == 92, arrived[k][:16, 384:].astype(F32), 0.0)
        filled += lax.shift_right_logical(jnp.max(first).astype(jnp.int32) + 15, 4) * 16
    x_s[pl.ds(pl.multiple_of(filled, 16), CHUNK_R)] = jnp.zeros((CHUNK_R, WIDE), BF16)
    chunks = lax.div(filled + CHUNK_R - 1, CHUNK_R)
    slot = lax.broadcasted_iota(jnp.int32, (1, ROWS), 1)
    codes_l[...] = jnp.where(slot < counts_ref[0], target_ref[...] + 1, 0).astype(F32)
    total[...] = total_l[...]

    def remote(c, carry):
        at = pl.ds(pl.multiple_of(c * CHUNK_R, CHUNK_R), CHUNK_R)
        x = x_s[at]
        tail = jnp.transpose(x[:, 384:].astype(F32))
        line = tail[90:91] * 32.0 + tail[91:92]
        codes_r[:, at] = line
        latent, slope_grid, slope, add = edge_forward(
            x, column(line), line, w_wide[...], w_half[...], query_ref[...]
        )
        latent_s[at] = latent
        slope_grid_s[at] = slope_grid
        slope_s[at] = slope
        total[...] += add
        return carry

    lax.fori_loop(0, chunks, remote, 0)

    lat_odd, mine = lax.rem(lax.axis_index("lat"), 2), lax.axis_index("core")
    from_down, from_up = swapped(lat_odd, arrived[4][SLOTS:], arrived[5][SLOTS:])
    sides[0], sides[1] = swapped(mine, arrived[6][SLOTS:], arrived[7][SLOTS:])
    row = lax.broadcasted_iota(jnp.int32, (MESH_B, 1), 0)
    mixed = mix[...]
    gains = gain[...]

    padded[0] = from_down
    padded[MESH_A + 1] = from_up

    def blend(u, carry):
        padded[u + 1] = (mixed * cot_ref[u].astype(F32)).astype(BF16).astype(F32)
        return carry

    lax.fori_loop(0, MESH_A, blend, 0)

    def spread(u, carry):
        here = padded[u + 1]
        left = jnp.where(row == 0, sides[0, pl.ds(u, 1)], pltpu.roll(here, 1, 0))
        right = jnp.where(row == MESH_B - 1, sides[1, pl.ds(u, 1)], pltpu.roll(here, MESH_B - 1, 0))
        sums = 0.25 * (padded[u + 2] + padded[u] + right + left)
        d_updated[pl.ds(pl.multiple_of(u * MESH_B, MESH_B), MESH_B)] = cot_ref[u].astype(F32) + sums
        return carry

    lax.fori_loop(0, MESH_A, spread, 0)

    def node(c, carry):
        at = pl.ds(pl.multiple_of(c * NODE_CHUNK, NODE_CHUNK), NODE_CHUNK)
        aggb = total[at].astype(BF16)
        aggb_s[at] = aggb
        hidden = dot(aggb, w_node[...])
        s = sigmoid(hidden)
        active = hidden * s
        centred = active - jnp.mean(active, axis=-1, keepdims=True)
        scale = lax.rsqrt(jnp.mean(centred * centred, axis=-1, keepdims=True) + LAYER_EPSILON)
        normed = centred * scale
        updated_out[at] = (mesh_ref[at].astype(F32) + normed * gains).astype(BF16)
        q = d_updated[at] * gains
        d_active = scale * (
            q
            - jnp.mean(q, axis=-1, keepdims=True)
            - normed * jnp.mean(q * normed, axis=-1, keepdims=True)
        )
        d_hidden = (d_active * (s * (1.0 + hidden * (1.0 - s)))).astype(BF16)
        d_hidden_s[at] = d_hidden
        d_agg[at] = (0.5 * dot(d_hidden, w_node[...], 1, 1)).astype(BF16)
        return carry

    lax.fori_loop(0, NODES // NODE_CHUNK, node, 0)
    rows = swapped(lat_odd, updated_out[:MESH_B], updated_out[NODES - MESH_B :])
    wide = updated_out[...].astype(F32).reshape(MESH_A, MESH_B, WIDE)
    columns = swapped(mine, wide[:, 0], wide[:, MESH_B - 1])
    for out, value in zip((row_1, row_2, column_1, column_2), rows + columns):
        out[...] = value.astype(BF16)
    d_query[...] = jnp.zeros((NODES, WIDE), F32)
    g_src[...] = jnp.zeros((WIDE, WIDE), F32)
    g_grid[...] = jnp.zeros((WIDE, WIDE), F32)

    def back(x_s, latent_s, slope_grid_s, slope_s, codes, size, c, carry):
        at = pl.ds(pl.multiple_of(c * size, size), size)
        line = codes[:, at]
        d_message = dot(hits(NODES, column(line) - 1.0, 1), d_agg[...])
        d_pre = (d_message * slope_s[at].astype(F32)).astype(BF16)
        d_query[...] += dot(hits(NODES, line - 1.0, 0), d_pre)
        g_src[...] += dot(d_pre, latent_s[at], 0, 0)
        d_latent = dot(d_pre, w_half[...], 1, 1)
        d_grid = (d_latent * slope_grid_s[at].astype(F32)).astype(BF16)
        g_grid[...] += dot(d_grid, x_s[at], 0, 0)
        return carry

    mine_s = (x_l, latent_l, slope_grid_l, slope_l, codes_l, CHUNK)
    theirs = (x_s, latent_s, slope_grid_s, slope_s, codes_r, CHUNK_R)
    lax.fori_loop(0, ROWS // CHUNK, functools.partial(back, *mine_s), 0)
    lax.fori_loop(0, chunks, functools.partial(back, *theirs), 0)

    def put(which, value):
        parts = value.reshape(16, 2, 16, WIDE)
        first, second = parts[:, 0], parts[:, 1]
        keep_out[:, which] = jnp.where(mine == 0, first, second).astype(BF16)
        send_out[:, which] = jnp.where(mine == 0, second, first).astype(BF16)

    put(0, g_grid[...])
    put(1, g_src[...])
    put(2, dot(d_query[...].astype(BF16), mesh_ref[...], 0, 0))
    put(3, dot(d_hidden_s[...], aggb_s[...], 0, 0))


def swapped(odd, first, second):
    first, second = first.astype(F32), second.astype(F32)
    return jnp.where(odd == 1, first, second), jnp.where(odd == 1, second, first)


def mix_kernel(updated_ref, mix, inner_out):
    row = lax.broadcasted_iota(jnp.int32, (MESH_B, 1), 0)
    quarter = 0.25 * mix[...]

    def line(u):
        return updated_ref[pl.ds(pl.multiple_of(u * MESH_B, MESH_B), MESH_B)].astype(F32)

    def step(u, carry):
        before, here = carry
        after = line(jnp.minimum(u + 1, MESH_A - 1))
        shown = jnp.where(u < MESH_A - 1, after, 0.0)
        left = jnp.where(row == 0, 0.0, pltpu.roll(here, 1, 0))
        right = jnp.where(row == MESH_B - 1, 0.0, pltpu.roll(here, MESH_B - 1, 0))
        inner_out[u] = here + quarter * (shown + before + right + left)
        return here, after

    lax.fori_loop(0, MESH_A, step, (jnp.zeros((MESH_B, WIDE), F32), line(0)))


def add_kernel(keep, got, out):
    out[...] = (keep[...].astype(F32) + got[...].astype(F32)).astype(BF16)


def finish_kernel(
    parts, inner, row_1, row_2, column_1, column_2, mix,
    mesh_out, g_grid, g_src, g_dst, g_node, row_s, side_s, sems,
):
    quarter = 0.25 * mix[...]
    last = MESH_B - 8
    middle = pl.ds(1, MESH_A - 2)
    stores = [
        pltpu.make_async_copy(
            inner.at[middle, pl.ds(8, MESH_B - 16)], mesh_out.at[middle, pl.ds(8, MESH_B - 16)], sems.at[0]
        )
    ]
    stores[0].start()
    rows = swapped(lax.rem(lax.axis_index("lat"), 2), row_1[...], row_2[...])
    sides = swapped(lax.axis_index("core"), column_1[...], column_2[...])
    place = lax.broadcasted_iota(jnp.int32, (8, 1), 0)
    for k, (at, edge) in enumerate(((0, 0), (last, 7))):
        side = quarter * sides[k]
        for u in range(MESH_A):
            side_s[k, u] = inner[u, at : at + 8] + jnp.where(place == edge, side[u : u + 1], 0.0)
        stores.append(
            pltpu.make_async_copy(side_s.at[k, middle], mesh_out.at[middle, pl.ds(at, 8)], sems.at[1 + k])
        )
        stores[-1].start()
    for k, u in enumerate((0, MESH_A - 1)):
        extra = quarter * rows[k]
        row_s[k] = inner[u] + extra
        row_s[k, :8] = side_s[0, u] + extra[:8]
        row_s[k, last:] = side_s[1, u] + extra[last:]
        stores.append(pltpu.make_async_copy(row_s.at[k], mesh_out.at[u], sems.at[3 + k]))
        stores[-1].start()
    for which, out in enumerate((g_grid, g_src, g_dst, g_node)):
        total = jnp.sum(parts[:, which].astype(F32), axis=0)
        out[...] = total[:, : out.shape[1]]
    for store in stores:
        store.wait()


def shape(*dims, dtype=BF16):
    return jax.ShapeDtypeStruct(dims, dtype)


def route(i, j):
    def step(kind, index):
        odd = index % 2
        return index + (0, 1 - 2 * odd, 2 * odd - 1)[kind]

    return [
        (a * LON + b, step(i, a) * LON + step(j, b) % LON)
        for a in range(LAT)
        for b in range(LON)
        if 0 <= step(i, a) < LAT
    ]


def moved(value, swap):
    return lax.ppermute(value, ("lat", "y", "core"), route(*swap))


def in_hbm(value):
    return pltpu.with_memory_space_constraint(value, pltpu.HBM)


def cost(flops, bytes_accessed):
    return pl.CostEstimate(flops=flops, bytes_accessed=bytes_accessed, transcendentals=0)


def call_send(*operands):
    return pl.pallas_call(
        send_kernel,
        out_shape=[shape(SLOTS + halo_rows(s), WIDE) for s in SWAPS]
        + [shape(WIDE, ROWS)]
        + [shape(*v.shape) for v in operands[6:]],
        in_specs=[pl.BlockSpec(memory_space=pltpu.HBM)] * 10,
        out_specs=[HBM] * len(SWAPS) + [VMEM] * 5,
        scratch_shapes=[
            pltpu.VMEM((4 * CHUNK_S, WIDE), BF16),
            pltpu.VMEM((2, MESH_B, WIDE), BF16),
            pltpu.VMEM((2, MESH_A, WIDE), BF16),
            pltpu.VMEM((8, 4 * CHUNK_S), F32),
            pltpu.VMEM((2, 128 * 8, 128), F32),
            pltpu.SMEM((1, PEERS), jnp.int32),
            pltpu.VMEM((CHANNELS, 8, 256), BF16),
            pltpu.VMEM((PEERS, SLOTS), jnp.int32),
            pltpu.VMEM((PEERS, SLOTS), jnp.int32),
            pltpu.VMEM((MESH_A, MESH_B, WIDE), BF16),
            pltpu.VMEM((1, WIDE), F32),
            pltpu.SemaphoreType.DMA((13,)),
            pltpu.SemaphoreType.DMA((12,)),
        ],
        name="send_rows",
        compiler_params=pltpu.CompilerParams(vmem_limit_bytes=SEND_LIMIT),
        cost_estimate=cost(5 * 10**9, 6 * 10**6),
    )(*(in_hbm(v) for v in operands))


def call_local(counts, feat, rows, target, bias, mesh, w_grid, w_src, w_dst):
    return pl.pallas_call(
        local_kernel,
        out_shape=[shape(ROWS, WIDE)] * 4 + [shape(NODES, WIDE, dtype=F32)] + [shape(NODES, WIDE)] * 3,
        in_specs=[SMEM] + [VMEM] * 8,
        out_specs=[VMEM] * 8,
        name="local_edges",
        compiler_params=pltpu.CompilerParams(vmem_limit_bytes=LOCAL_LIMIT * 2**20),
        cost_estimate=cost(9 * 10**9, 14 * 10**6),
    )(counts, feat, rows, target, bias, mesh, w_grid, w_src, w_dst)


def call_main(arrived, local, counts, target, mesh, cotangent, w_node, gain, mix):
    big = pltpu.VMEM((2 * CHUNK_R, WIDE), BF16)
    square = pltpu.VMEM((WIDE, WIDE), F32)
    square_b = pltpu.VMEM((WIDE, WIDE), BF16)
    line = pltpu.VMEM((1, ROWS), F32)
    line_r = pltpu.VMEM((1, 2 * CHUNK_R), F32)
    return pl.pallas_call(
        main_kernel,
        out_shape=[shape(16, 4, 16, WIDE)] * 2
        + [shape(NODES, WIDE), shape(MESH_B, WIDE), shape(MESH_B, WIDE)]
        + [shape(MESH_A, WIDE), shape(MESH_A, WIDE)],
        in_specs=[VMEM] * 16 + [SMEM] + [VMEM] * 6,
        out_specs=[VMEM] * 7,
        scratch_shapes=[
            pltpu.VMEM((ROWS + CHUNK_R, WIDE), BF16), big, big, big, square,
            line, line_r, square, square_b,
            square_b, square_b, square, square, square, pltpu.VMEM((MESH_A + 2, MESH_B, WIDE), F32),
            pltpu.VMEM((2, MESH_A, WIDE), F32),
        ],
        name="nodes_and_back",
        compiler_params=pltpu.CompilerParams(vmem_limit_bytes=MAIN_LIMIT * 2**20),
        cost_estimate=cost(16 * 10**9, 20 * 10**6),
    )(*arrived, *local, counts, target, mesh, cotangent, w_node, gain, mix)


def small(limit):
    return pltpu.CompilerParams(vmem_limit_bytes=limit * 2**20)


def call_mix(updated, mix):
    return pl.pallas_call(
        mix_kernel,
        out_shape=shape(MESH_A, MESH_B, WIDE, dtype=F32),
        in_specs=[VMEM] * 2,
        out_specs=VMEM,
        name="mix",
        compiler_params=small(4),
        cost_estimate=cost(10**7, 2 * 10**6),
    )(updated, mix)


def call_add(keep, got):
    return pl.pallas_call(
        add_kernel,
        out_shape=shape(*keep.shape),
        in_specs=[VMEM] * 2,
        out_specs=VMEM,
        name="add_pair",
        compiler_params=small(4),
        cost_estimate=cost(10**6, 3 * 10**6),
    )(keep, got)


def call_finish(parts, inner, row_1, row_2, column_1, column_2, mix):
    return pl.pallas_call(
        finish_kernel,
        out_shape=[shape(MESH_A, MESH_B, WIDE, dtype=F32), shape(16, CHANNELS, dtype=F32)]
        + [shape(16, WIDE, dtype=F32)] * 3,
        in_specs=[VMEM] * 7,
        out_specs=[HBM] + [VMEM] * 4,
        scratch_shapes=[
            pltpu.VMEM((2, MESH_B, WIDE), F32),
            pltpu.VMEM((2, MESH_A, 8, WIDE), F32),
            pltpu.SemaphoreType.DMA((5,)),
        ],
        name="finish",
        compiler_params=small(8),
    )(parts, inner, row_1, row_2, column_1, column_2, mix)


def on_device(
    grid_feat, mesh_in, w_grid, w_src, w_dst, b_edge, w_node, node_gain, mix_gain,
    send_rows, send_target, send_counts, local_rows, local_target, local_counts, cotangent,
):
    feat = jnp.transpose(grid_feat, (2, 0, 1))
    mesh = mesh_in.reshape(NODES, WIDE)
    mix = mix_gain.reshape(1, WIDE)
    gain = node_gain.reshape(1, WIDE)
    bias = b_edge.reshape(1, WIDE)
    *sends, flat, mesh_v, w_grid, w_src, w_dst = call_send(
        send_counts, feat, send_rows[0], send_target[0], cotangent, mix, mesh, w_grid, w_src, w_dst
    )
    arrived = [moved(value, step) for value, step in zip(sends, SWAPS)]
    local = call_local(local_counts, flat, local_rows, local_target, bias, mesh_v, w_grid, w_src, w_dst)
    keep, send, updated, *halos = call_main(
        arrived, local, local_counts, local_target, mesh, cotangent, w_node, gain, mix
    )
    got = lax.ppermute(send, ("core",), [(0, 1), (1, 0)])
    halos = [moved(v, swap) for v, swap in zip(halos, ((1, 0), (2, 0), (0, 1), (0, 2)))]
    both = call_add(keep, got)
    parts = lax.all_to_all(both.reshape(16, 64, WIDE), ("lat", "y"), 0, 0, tiled=True)
    mesh_out, *sums = call_finish(parts.reshape(16, 4, 16, WIDE), call_mix(updated, mix), *halos, mix)
    return (mesh_out,) + tuple(g.T for g in sums)


def solution(mesh):
    fine = jax.sharding.Mesh(mesh.devices.reshape(4, LAT, LON // 2, 2), ("dp", "lat", "y", "core"))
    lists = ("dp", "lat", "y", "core")
    tiles = P(("dp", "lat"), ("y", "core"), None)
    return jax.shard_map(
        on_device,
        mesh=fine,
        in_specs=(
            tiles, tiles, P(), P(), P(), P(), P(), P(), P(),
            P(lists, None, None), P(lists, None, None), P(lists, None),
            P(lists, None), P(lists, None), P(lists), tiles,
        ),
        out_specs=(tiles,) + (P("dp", ("lat", "y", "core")),) * 4,
        check_vma=False,
    )
```
